256 devices in a mesh: ctx: 64 (over y, z, core), head: 4 (over x).
Axes of the slice: x: 4, y: 4, z: 8, core: 2. Of those that a mesh axis runs over, the one named last changes fastest.
Arguments:
- queries: bfloat16 [32256, 4096], P('ctx', 'head'), may hold values from -6 to 6
- keys: bfloat16 [32256, 4096], P('ctx', 'head'), may hold values from -6 to 6
- values: bfloat16 [32256, 4096], P('ctx', 'head'), may hold values from -6 to 6
- out_weight: bfloat16 [4096, 4096], P('head'), may hold values from -0.09375 to 0.09375
- norm_gain: float32 [4096], P('head'), may hold values from 0.1 to 1.9
- tile_counts: int32 [64], replicated, may hold values from 1 to 63, as said below
- route_device: int32 [4032], P('ctx'), may hold values from -1 to 63, as said below
- route_slot: int32 [4032], P('ctx'), may hold values from -1 to 31, as said below
- session_starts: int32 [4], replicated, may hold values from 0 to 16383, as said below
Outputs:
- balanced_out: bfloat16 [16384, 4096], P('ctx', 'head')
The draws below stay inside these ranges and needn't reach their ends.
Inputs may be any that keep to these rules, and one draw needn't show every extreme that they name: `tile_counts`: each value is at least 1 and the values sum to 2048; some index has exactly 63 live tiles. `route_device`: the live tiles of an index are its first tile_counts slots; dead slots hold -1; each index of ctx receives exactly 32 tiles, and no index sends more than 1 tiles to one index. `route_slot`: dead slots hold -1; every pair of receiving index and slot below 32 is named by exactly one live tile. `session_starts`: strictly increasing, first value 0, last value 16384 - 1.
All inputs are finite; a program needn't handle non-finite values.
Results may differ from the reference program's by a relative error of at most 0.018.
Values may be sent and summed in bfloat16 or wider, within the bound.
No kernel may reach another device: no remote copies, remote signals or barrier semaphores. Data moves between devices by JAX's collectives and lax.ppermute only.
A program may use at most 128 MiB of HBM per device.

```python
import jax
import jax.numpy as jnp
from jax import lax

D = 4096
HEADS = 32
DH = 128
CH = 8
BAL = 32
SESSIONS = 4
SLOTS = 63
ROWS = 32256
LIVE = 16384
N_CTX = 64
N_HEAD = 4


def counts_helper(key):
    ordering = jax.random.permutation(jax.random.fold_in(key, 11), N_CTX)
    spread = jax.random.randint(jax.random.fold_in(key, 12), (N_CTX // 2,), 0, BAL)
    spread = spread.at[0].set(BAL - 1)
    counts = jnp.zeros((N_CTX,), jnp.int32)
    counts = counts.at[ordering[0::2]].set(BAL + spread)
    counts = counts.at[ordering[1::2]].set(BAL - spread)
    return counts.astype(jnp.int32)


def route_helper(key):
    counts = counts_helper(key)
    first = jnp.cumsum(counts) - counts
    column = jnp.arange(SLOTS, dtype=jnp.int32)[None, :]
    global_index = first[:, None] + column
    is_live = column < counts[:, None]
    shuffle = jax.random.permutation(jax.random.fold_in(key, 13), N_CTX).astype(jnp.int32)
    device = jnp.where(is_live, shuffle[global_index % N_CTX], -1)
    row_keys = jax.random.split(jax.random.fold_in(key, 15), N_CTX)
    slot_orders = jax.vmap(lambda one_key: jax.random.permutation(one_key, BAL))(row_keys).astype(jnp.int32)
    safe_device = jnp.maximum(device, 0)
    safe_rank = jnp.minimum(global_index // N_CTX, BAL - 1)
    target = jnp.where(is_live, slot_orders[safe_device, safe_rank], -1)
    return (device.reshape(-1).astype(jnp.int32), target.reshape(-1).astype(jnp.int32))


def draw_tile_counts(key, part):
    return counts_helper(key)


def draw_route_device(key, part):
    return route_helper(key)[0]


def draw_route_slot(key, part):
    return route_helper(key)[1]


def draw_session_starts(key, part):
    picks = jax.random.permutation(jax.random.fold_in(key, 14), LIVE - 2)[:SESSIONS - 2] + 1
    middle = jnp.sort(picks).astype(jnp.int32)
    return jnp.concatenate([jnp.zeros((1,), jnp.int32), middle, jnp.full((1,), LIVE - 1, jnp.int32)]).astype(jnp.int32)


def shard_levels(own_key, shape, pieces, smallest, high):
    def one(position, shards_of):
        heights = jax.random.uniform(jax.random.fold_in(jax.random.fold_in(own_key, 6), position), (shards_of,), jnp.float32, smallest / len(pieces), high / len(pieces))
        return jnp.repeat(jnp.exp(heights), shape[position] // shards_of).reshape((-1,) + (1,) * (len(shape) - position - 1))

    level = one(*pieces[0])
    for cut in pieces[1:]:
        level = level * one(*cut)
    return level


def bell_draw(stream_key, shape, scale, bound, shards=(), held_as=jnp.bfloat16):
    loudness = shard_levels(stream_key, shape, shards, -0.22, 0.18) if shards else 1.0
    entries = jax.random.normal(stream_key, shape, jnp.float32) * scale * loudness
    return jnp.minimum(jnp.maximum(entries, -bound), bound).astype(held_as)


def setup_inputs(seed: int = 0) -> dict:
    arg_keys = jax.random.split(jax.random.key(seed), 10)
    queries = bell_draw(arg_keys[0], (ROWS, D), 1.0, 6.0, ((0, 64), (1, 4)))
    keys = bell_draw(arg_keys[1], (ROWS, D), 1.0, 6.0, ((0, 64), (1, 4)))
    values = bell_draw(arg_keys[2], (ROWS, D), 1.0, 6.0, ((0, 64), (1, 4)))
    out_weight = bell_draw(arg_keys[3], (D, D), D ** -0.5, 0.09375, ((0, 4),))
    norm_gain = jnp.clip(1.0 + 0.18 * jax.random.normal(arg_keys[4], (D,), jnp.float32), 0.1, 1.9)
    tile_counts = draw_tile_counts(jax.random.fold_in(arg_keys[9], 71), 0)
    route_device = draw_route_device(jax.random.fold_in(arg_keys[9], 71), 0)
    route_slot = draw_route_slot(jax.random.fold_in(arg_keys[9], 71), 0)
    session_starts = draw_session_starts(jax.random.fold_in(arg_keys[9], 71), 0)
    return {"queries": queries, "keys": keys, "values": values, "out_weight": out_weight, "norm_gain": norm_gain, "tile_counts": tile_counts, "route_device": route_device, "route_slot": route_slot, "session_starts": session_starts}


EPSILON = 1e-06

def feature(block):
    value = block.astype(jnp.float32)
    return jnp.where(value > 0, value + 1.0, jnp.exp(jnp.minimum(value, 0.0))).astype(jnp.bfloat16)

def reference(queries, keys, values, out_weight, norm_gain, tile_counts, route_device, route_slot, session_starts):
    tile_total = N_CTX * SLOTS
    query_feature_map = feature(queries).reshape(tile_total, CH, HEADS, DH)
    key_map = feature(keys).reshape(tile_total, CH, HEADS, DH)
    value_row_block = values.reshape(tile_total, CH, HEADS, DH)
    first_tile = (jnp.cumsum(tile_counts) - tile_counts).astype(jnp.int32)
    tile_ids = jnp.arange(tile_total, dtype=jnp.int32)
    tile_dev = tile_ids // SLOTS
    tile_col = tile_ids % SLOTS
    tile_live = tile_col < tile_counts[tile_dev]
    positions = (CH * (first_tile[tile_dev] + tile_col))[:, None] + jnp.arange(CH, dtype=jnp.int32)[None, :]
    sessions = (lax.optimization_barrier(jnp.sum((session_starts[None, None, :] <= positions[:, :, None]).astype(jnp.int32), axis=2)) - 1).astype(jnp.int32)
    causal = jnp.arange(CH)[None, :] <= jnp.arange(CH)[:, None]

    def advance(carried, inputs):
        key_value_state, carry_sess = carried
        q_tile, k_tile, v_tile, s_tile, l_tile = inputs
        query_float = q_tile.astype(jnp.float32)
        k_float = k_tile.astype(jnp.float32)
        value_float = v_tile.astype(jnp.float32)
        allowed = causal & (s_tile[None, :] == s_tile[:, None])
        scores = jnp.einsum('thd,shd->hts', query_float, k_float, precision=lax.Precision.HIGHEST)
        scores = jnp.where(allowed[None], scores, 0.0)
        inside = jnp.einsum('hts,shd->thd', scores, value_float, precision=lax.Precision.HIGHEST)
        carried_portion = jnp.einsum('ycu,cux->ycx', query_float, key_value_state, precision=lax.Precision.HIGHEST)
        carried_portion = jnp.where((s_tile == carry_sess)[:, None, None], carried_portion, 0.0)
        numerator = inside + carried_portion
        last_sess = s_tile[CH - 1]
        selected_rows = jnp.where((s_tile == last_sess)[:, None, None], k_float, 0.0)
        appended_term = jnp.einsum('pld,plw->ldw', selected_rows, value_float, precision=lax.Precision.HIGHEST)
        new_state = jnp.where(carry_sess == last_sess, key_value_state, 0.0) + appended_term
        key_value_state = jnp.where(l_tile, new_state, key_value_state)
        carry_sess = jnp.where(l_tile, last_sess, carry_sess).astype(jnp.int32)
        return ((key_value_state, carry_sess), numerator)
    initial = (jnp.zeros((HEADS, DH, DH), jnp.float32), jnp.array(-1, jnp.int32))
    _, numerators = lax.scan(advance, initial, (query_feature_map, key_map, value_row_block, sessions, tile_live))
    inverse_rms = lax.rsqrt(lax.optimization_barrier(jnp.mean(numerators * numerators, axis=-1, keepdims=True)) + EPSILON)
    attended = (numerators * inverse_rms * norm_gain.reshape(HEADS, DH)).astype(jnp.bfloat16).reshape(tile_total, CH, D)
    destination = jnp.where(route_device >= 0, route_device * BAL + route_slot, N_CTX * BAL).astype(jnp.int32)
    balanced = jnp.zeros((N_CTX * BAL, CH, D), jnp.bfloat16).at[destination].set(attended, mode='drop')
    balanced = balanced.reshape(N_CTX * BAL * CH, D)
    group_width = D // N_HEAD
    summed = jnp.zeros((N_CTX * BAL * CH, D), jnp.float32)
    for group_index in range(N_HEAD):
        lower = group_index * group_width
        partial_value = jnp.dot(balanced[:, lower:lower + group_width].astype(jnp.float32), out_weight[lower:lower + group_width].astype(jnp.float32), precision=lax.Precision.HIGHEST)
        summed = summed + partial_value.astype(jnp.bfloat16).astype(jnp.float32)
    return summed.astype(jnp.bfloat16)
```

```python
import jax
import jax.numpy as jnp
from jax import lax
from jax.experimental import pallas as pl
from jax.experimental.pallas import tpu as pltpu
from jax.sharding import PartitionSpec as P

DH = 128
CH = 8
BAL = 32
EPSILON = 1e-06
FAR = 1 << 28


def feature(block):
    value = block.astype(jnp.float32)
    return jnp.where(value > 0, value + 1.0, jnp.exp(jnp.minimum(value, 0.0))).astype(jnp.bfloat16)


def entry_kernel(info, keys, values, out):
    row = lax.broadcasted_iota(jnp.int32, keys.shape, 0)
    kept = (row >= info[0]) & (row < info[1])
    phi = jnp.where(kept, feature(keys[...]).astype(jnp.float32), 0.0).astype(jnp.bfloat16)
    out[0] = lax.dot_general(
        phi, values[...], (((0,), (0,)), ((), ())), preferred_element_type=jnp.float32
    ).astype(jnp.bfloat16)


def inside_kernel(info, queries, keys, values, phi_out, out):
    rows = queries.shape[0]
    row = lax.broadcasted_iota(jnp.int32, (rows, 1), 0)
    lower = jnp.full((rows, 1), -FAR, jnp.int32)
    for b in range(4):
        lower = jnp.maximum(lower, jnp.where(row >= info[3 + b], info[3 + b], -FAR))
    column = lax.broadcasted_iota(jnp.int32, (rows, rows), 1)
    allowed = (column <= row) & (column >= lower)
    phi_q = feature(queries[...])
    phi_k = feature(keys[...])
    phi_out[...] = phi_q
    scores = lax.dot_general(
        phi_q, phi_k, (((1,), (1,)), ((), ())), preferred_element_type=jnp.float32
    )
    scores = jnp.where(allowed, scores, 0.0).astype(jnp.bfloat16)
    out[...] = jnp.dot(scores, values[...], preferred_element_type=jnp.float32)


def attend_kernel(info, targets, phi_q, inside, state, gain, out, scratch):
    rows = phi_q.shape[0]
    carried = jnp.dot(phi_q[...], state[0], preferred_element_type=jnp.float32)
    row = lax.broadcasted_iota(jnp.int32, (rows, 1), 0)
    numer = inside[...] + jnp.where(row < info[2], carried, 0.0)
    inverse = lax.rsqrt(jnp.mean(numer * numer, axis=1, keepdims=True) + EPSILON)
    scratch[...] = numer * inverse * gain[...]
    for j in range(rows // CH):
        target = targets[j]

        @pl.when(target >= 0)
        def _():
            out[target] = scratch[CH * j : CH * (j + 1), :].astype(jnp.bfloat16)


def project_kernel(slots, arrived, weight, out, gathered, packed):
    @pl.when(pl.program_id(0) == 0)
    def _():
        for s in range(arrived.shape[0]):
            slot = slots[s]

            @pl.when(slot >= 0)
            def _():
                start = pl.multiple_of(slot * CH, CH)
                gathered[pl.ds(start, CH), :] = arrived[s].astype(jnp.float32)

        packed[...] = gathered[...].astype(jnp.bfloat16)

    out[...] = jnp.dot(packed[...], weight[...], preferred_element_type=jnp.float32).astype(
        jnp.bfloat16
    )


def ctx_exchange(x):
    return lax.all_to_all(x, "ctx", split_axis=0, concat_axis=0, tiled=True)


def per_device(
    queries,
    keys,
    values,
    out_weight,
    norm_gain,
    tile_counts,
    route_device,
    route_slot,
    session_starts,
):
    ranks = lax.axis_size("ctx")
    here = lax.axis_index("ctx")
    rows, width = queries.shape
    heads = width // DH
    tiles = rows // CH

    ids = jnp.arange(ranks, dtype=jnp.int32)
    first = CH * jnp.sum(jnp.where(ids[None, :] < ids[:, None], tile_counts[None, :], 0), axis=1)
    after = first + CH * tile_counts
    before_sess = jnp.sum((session_starts[None, :] <= first[:, None] - 1).astype(jnp.int32), axis=1)
    last_sess = jnp.sum((session_starts[None, :] <= after[:, None] - 1).astype(jnp.int32), axis=1)
    mine = ids == here
    offset = jnp.sum(jnp.where(mine, first, 0))
    live = jnp.sum(jnp.where(mine, after - first, 0))
    local_starts = session_starts - offset
    last_start = jnp.max(jnp.where(local_starts <= live - 1, local_starts, -FAR))
    next_start = jnp.min(jnp.where(local_starts >= 0, local_starts, FAR))
    info = jnp.concatenate([jnp.stack([last_start, live, next_start]), local_starts]).astype(
        jnp.int32
    )

    part = heads * DH // ranks
    wide = ranks * part
    step = jnp.arange(wide, dtype=jnp.int32)
    group = step // part
    prior = jnp.repeat(before_sess, part)
    last = jnp.repeat(last_sess, part)
    prefix = (
        (step[:, None] % part == step[None, :] % part)
        & (group[None, :] < group[:, None])
        & (last[None, :] == prior[:, None])
    ).astype(jnp.bfloat16)

    column = lambda h, *_: (0, h)
    entry = pl.pallas_call(
        entry_kernel,
        grid_spec=pltpu.PrefetchScalarGridSpec(
            num_scalar_prefetch=1,
            grid=(heads,),
            in_specs=[pl.BlockSpec((rows, DH), column), pl.BlockSpec((rows, DH), column)],
            out_specs=pl.BlockSpec((1, DH, DH), lambda h, *_: (h, 0, 0)),
        ),
        out_shape=jax.ShapeDtypeStruct((heads, DH, DH), jnp.bfloat16),
        name="entry",
    )(info, keys, values)

    sent = entry.reshape(ranks, part, DH)
    got = ctx_exchange(sent)

    phi_q, inside = pl.pallas_call(
        inside_kernel,
        grid_spec=pltpu.PrefetchScalarGridSpec(
            num_scalar_prefetch=1,
            grid=(heads,),
            in_specs=[pl.BlockSpec((rows, DH), column)] * 3,
            out_specs=[pl.BlockSpec((rows, DH), column)] * 2,
        ),
        out_shape=[
            jax.ShapeDtypeStruct((rows, width), jnp.bfloat16),
            jax.ShapeDtypeStruct((rows, width), jnp.float32),
        ],
        name="inside",
    )(info, queries, keys, values)

    chosen = ids[:, None] == route_device[None, :]
    labels = jnp.sum(jnp.where(chosen, route_slot[None, :] + 1, 0), axis=1) - 1
    slots = ctx_exchange(labels.astype(jnp.int32))

    summed = jnp.dot(prefix, got.reshape(wide, DH), preferred_element_type=jnp.float32)
    state = ctx_exchange(summed.astype(jnp.bfloat16).reshape(ranks, part, DH))
    state = state.reshape(heads, DH, DH)

    payload = pl.pallas_call(
        attend_kernel,
        grid_spec=pltpu.PrefetchScalarGridSpec(
            num_scalar_prefetch=2,
            grid=(heads,),
            in_specs=[
                pl.BlockSpec((rows, DH), column),
                pl.BlockSpec((rows, DH), column),
                pl.BlockSpec((1, DH, DH), lambda h, *_: (h, 0, 0)),
                pl.BlockSpec((1, DH), column),
            ],
            out_specs=pl.BlockSpec((ranks, CH, DH), lambda h, *_: (0, 0, h)),
            scratch_shapes=[pltpu.VMEM((rows, DH), jnp.float32)],
        ),
        out_shape=jax.ShapeDtypeStruct((ranks, CH, width), jnp.bfloat16),
        name="attend",
    )(info, route_device, phi_q, inside, state, norm_gain.reshape(1, width))

    arrived = ctx_exchange(payload)

    model = out_weight.shape[1]
    block = 1024
    partial = pl.pallas_call(
        project_kernel,
        grid_spec=pltpu.PrefetchScalarGridSpec(
            num_scalar_prefetch=1,
            grid=(model // block,),
            in_specs=[
                pl.BlockSpec((ranks, CH, width), lambda n, *_: (0, 0, 0)),
                pl.BlockSpec((width, block), lambda n, *_: (0, n)),
            ],
            out_specs=pl.BlockSpec((BAL * CH, block), lambda n, *_: (0, n)),
            scratch_shapes=[
                pltpu.VMEM((BAL * CH, width), jnp.float32),
                pltpu.VMEM((BAL * CH, width), jnp.bfloat16),
            ],
        ),
        out_shape=jax.ShapeDtypeStruct((BAL * CH, model), jnp.bfloat16),
        name="project",
    )(slots, arrived, out_weight)
    return lax.psum_scatter(partial, "head", scatter_dimension=1, tiled=True)


def solution(mesh):
    placed = (
        P("ctx", "head"),
        P("ctx", "head"),
        P("ctx", "head"),
        P("head", None),
        P("head"),
        P(),
        P("ctx"),
        P("ctx"),
        P(),
    )
    return jax.shard_map(
        per_device, mesh=mesh, in_specs=placed, out_specs=P("ctx", "head"), check_vma=False
    )
```

```python
import jax
import jax.numpy as jnp
from jax import lax
from jax.experimental import pallas as pl
from jax.experimental.pallas import tpu as pltpu
from jax.sharding import PartitionSpec as P

DH = 128
CH = 8
BAL = 32
SESSIONS = 4
EPSILON = 1e-06
FAR = 1 << 28
SMEM = pltpu.MemorySpace.SMEM
VMEM = pltpu.MemorySpace.VMEM
HBM = pltpu.MemorySpace.HBM


def feature(block):
    value = block.astype(jnp.float32)
    return jnp.where(value > 0, value + 1.0, jnp.exp(jnp.minimum(value, 0.0))).astype(jnp.bfloat16)


def entry_kernel(counts, starts, device, slot, keys_hbm, values_hbm, out, info, keys, values, done):
    ranks = counts.shape[0]
    here = lax.axis_index("ctx")
    rows, width = keys.shape
    part = width // ranks
    copies = []
    for h in range(width // DH):
        columns = slice(DH * h, DH * (h + 1))
        pair = [
            pltpu.make_async_copy(source.at[:, columns], held.at[:, columns], done.at[i, h])
            for i, (source, held) in enumerate(((keys_hbm, keys), (values_hbm, values)))
        ]
        copies.append(pair)
        for copy in pair:
            copy.start()

    def add(k, total):
        return total + jnp.where(k < here, counts[k], 0)

    offset = CH * lax.fori_loop(0, ranks, add, jnp.int32(0), unroll=8)
    live = CH * counts[here]
    last_start = jnp.int32(-FAR)
    next_start = jnp.int32(FAR)
    for b in range(SESSIONS):
        local = starts[b] - offset
        info[3 + b] = local
        last_start = jnp.maximum(last_start, jnp.where(local <= live - 1, local, -FAR))
        next_start = jnp.minimum(next_start, jnp.where(local >= 0, local, FAR))
    info[0] = last_start
    info[1] = live
    info[2] = next_start
    info[7] = counts[here]

    out[:, part:, :] = jnp.full((ranks, out.shape[1] - part, DH), -1.0, jnp.bfloat16)

    def mark(j, carry):
        value = jnp.full((out.shape[1] - part, DH), slot[j], jnp.int32)
        out[device[j], part:, :] = value.astype(jnp.float32).astype(jnp.bfloat16)
        return carry

    lax.fori_loop(0, counts[here], mark, 0)

    row = lax.broadcasted_iota(jnp.int32, (rows, DH), 0)
    kept = (row >= last_start) & (row < live)
    each = DH // part
    for h in range(width // DH):
        columns = slice(DH * h, DH * (h + 1))
        for copy in copies[h]:
            copy.wait()
        phi = jnp.where(kept, feature(keys[:, columns]).astype(jnp.float32), 0.0)
        state = lax.dot_general(
            phi.astype(jnp.bfloat16),
            values[:, columns],
            (((0,), (0,)), ((), ())),
            preferred_element_type=jnp.float32,
        ).astype(jnp.bfloat16)
        for i in range(each):
            out[each * h + i, :part, :] = state[part * i : part * (i + 1), :]


def prefix_kernel(counts, starts, got, out):
    ranks, part, _ = out.shape
    running = jnp.zeros((part, DH), jnp.float32)
    first = jnp.int32(0)
    for k in range(ranks):
        out[k] = running.astype(jnp.bfloat16)
        after = first + CH * counts[k]
        reset = jnp.int32(0)
        for b in range(SESSIONS):
            reset = reset | ((starts[b] >= first) & (starts[b] < after)).astype(jnp.int32)
        first = after
        if k + 1 < ranks:
            keep = jnp.full((part, DH), 1 - reset, jnp.int32) > 0
            running = jnp.where(keep, running, 0.0) + got[k, :part, :].astype(jnp.float32)


def inside_kernel(info, queries, keys, values, phi_out, out):
    rows, width = queries.shape
    row = lax.broadcasted_iota(jnp.int32, (rows, 1), 0)
    lower = jnp.full((rows, 1), -FAR, jnp.int32)
    for b in range(SESSIONS):
        lower = jnp.maximum(lower, jnp.where(row >= info[3 + b], info[3 + b], -FAR))
    column = lax.broadcasted_iota(jnp.int32, (rows, rows), 1)
    allowed = (column <= row) & (column >= lower)
    for h in range(width // DH):
        columns = slice(DH * h, DH * (h + 1))
        phi_q = feature(queries[:, columns])
        phi_k = feature(keys[:, columns])
        phi_out[:, columns] = phi_q
        scores = lax.dot_general(
            phi_q, phi_k, (((1,), (1,)), ((), ())), preferred_element_type=jnp.float32
        )
        scores = jnp.where(allowed, scores, 0.0).astype(jnp.bfloat16)
        out[:, columns] = jnp.dot(
            scores, values[:, columns], preferred_element_type=jnp.float32
        )


def attend_kernel(info, device, phi_q, inside, state, gain, out, scratch):
    rows, width = phi_q.shape
    row = lax.broadcasted_iota(jnp.int32, (rows, 1), 0)
    open_row = row < info[2]
    for h in range(width // DH):
        columns = slice(DH * h, DH * (h + 1))
        carried = jnp.dot(phi_q[:, columns], state[h], preferred_element_type=jnp.float32)
        numer = inside[:, columns] + jnp.where(open_row, carried, 0.0)
        inverse = lax.rsqrt(jnp.mean(numer * numer, axis=1, keepdims=True) + EPSILON)
        scratch[:, columns] = numer * inverse * gain[:, columns]

    def place(j, carry):
        start = pl.multiple_of(j * CH, CH)
        out[device[j]] = scratch[pl.ds(start, CH), :].astype(jnp.bfloat16)
        return carry

    lax.fori_loop(0, info[7], place, 0)


def column_copies(weight, held, done, shifts):
    groups = lax.axis_size("head")
    block = weight.shape[1] // groups
    half = block // 2
    copies = []
    for by in shifts:
        column = lax.rem(lax.axis_index("head") + by, groups)
        for i in range(2):
            start = pl.multiple_of(column * block + i * half, half)
            n = len(copies)
            copies.append(
                pltpu.make_async_copy(weight.at[:, pl.ds(start, half)], held.at[n], done.at[n])
            )
    for copy in copies:
        copy.start()
    return copies


def products(packed, held, copies, outs):
    for n, (copy, out) in enumerate(zip(copies, outs)):
        copy.wait()
        out[...] = jnp.dot(packed[...], held[n], preferred_element_type=jnp.float32).astype(
            jnp.bfloat16
        )


def across_kernel(slots, arrived, weight, packed, left, right, gathered, held, done):
    copies = column_copies(weight, held, done, (2,))
    for s in range(arrived.shape[0]):
        slot = slots[s]

        @pl.when(slot >= 0)
        def _():
            start = pl.multiple_of(slot * CH, CH)
            gathered[pl.ds(start, CH), :] = arrived[s].astype(jnp.float32)

    packed[...] = gathered[...].astype(jnp.bfloat16)
    products(packed, held, copies, (left, right))


def beside_kernel(packed, weight, ahead_left, ahead_right, behind_left, behind_right, held, done):
    copies = column_copies(weight, held, done, (1, lax.axis_size("head") - 1))
    products(packed, held, copies, (ahead_left, ahead_right, behind_left, behind_right))


def own_kernel(packed, weight, left, right, held, done):
    copies = column_copies(weight, held, done, (0,))
    products(packed, held, copies, (left, right))


def ctx_exchange(x):
    return lax.all_to_all(x, "ctx", split_axis=0, concat_axis=0, tiled=True)


def head_shift(x, by):
    count = lax.axis_size("head")
    return lax.ppermute(x, "head", [(i, (i + by) % count) for i in range(count)])


def wide(x):
    return x.astype(jnp.float32)


def reduce_heads(across, ahead, behind, own):
    up = head_shift(across[0], 1)
    down = head_shift(across[1], -1)
    ahead_right = head_shift(ahead[1], 1)
    behind_left = head_shift(behind[0], -1)
    ahead_left = head_shift((wide(ahead[0]) + wide(up)).astype(jnp.bfloat16), 1)
    behind_right = head_shift((wide(behind[1]) + wide(down)).astype(jnp.bfloat16), -1)
    left = wide(own[0]) + wide(ahead_left) + wide(behind_left)
    right = wide(own[1]) + wide(ahead_right) + wide(behind_right)
    return jnp.concatenate([left, right], axis=1).astype(jnp.bfloat16)


def per_device(
    queries,
    keys,
    values,
    out_weight,
    norm_gain,
    tile_counts,
    route_device,
    route_slot,
    session_starts,
):
    ranks = lax.axis_size("ctx")
    groups = lax.axis_size("head")
    rows, width = queries.shape
    heads = width // DH
    part = heads * DH // ranks
    smem = pl.BlockSpec(memory_space=SMEM)
    vmem = pl.BlockSpec(memory_space=VMEM)
    hbm = pl.BlockSpec(memory_space=HBM)
    in_hbm = lambda x: pltpu.with_memory_space_constraint(x, HBM)
    params = pltpu.CompilerParams(vmem_limit_bytes=16 << 20)

    tile_counts, session_starts, route_device, route_slot = map(
        in_hbm, (tile_counts, session_starts, route_device, route_slot)
    )
    entry, info = pl.pallas_call(
        entry_kernel,
        in_specs=[smem] * 4 + [hbm] * 2,
        out_specs=[vmem, smem],
        out_shape=[
            jax.ShapeDtypeStruct((ranks, part + 8, DH), jnp.bfloat16),
            jax.ShapeDtypeStruct((8,), jnp.int32),
        ],
        scratch_shapes=[
            pltpu.VMEM((rows, width), keys.dtype),
            pltpu.VMEM((rows, width), values.dtype),
            pltpu.SemaphoreType.DMA((2, heads)),
        ],
        compiler_params=params,
        name="entry",
    )(tile_counts, session_starts, route_device, route_slot, in_hbm(keys), in_hbm(values))

    got = ctx_exchange(entry)

    phi_q, inside = pl.pallas_call(
        inside_kernel,
        in_specs=[smem] + [vmem] * 3,
        out_specs=[vmem] * 2,
        out_shape=[
            jax.ShapeDtypeStruct((rows, width), jnp.bfloat16),
            jax.ShapeDtypeStruct((rows, width), jnp.float32),
        ],
        compiler_params=params,
        name="inside",
    )(info, queries, keys, values)

    got, phi_q, inside = lax.optimization_barrier((got, phi_q, inside))
    slots = got[:, part, 0].astype(jnp.int32)
    got, slots = lax.optimization_barrier((got, slots))
    summed = pl.pallas_call(
        prefix_kernel,
        in_specs=[smem, smem, vmem],
        out_specs=vmem,
        out_shape=jax.ShapeDtypeStruct((ranks, part, DH), jnp.bfloat16),
        compiler_params=params,
        name="prefix",
    )(tile_counts, session_starts, got)

    state = ctx_exchange(summed).reshape(heads, DH, DH)

    payload = pl.pallas_call(
        attend_kernel,
        in_specs=[smem] * 2 + [vmem] * 4,
        out_specs=vmem,
        out_shape=jax.ShapeDtypeStruct((ranks, CH, width), jnp.bfloat16),
        scratch_shapes=[pltpu.VMEM((rows, width), jnp.float32)],
        compiler_params=params,
        name="attend",
    )(info, route_device, phi_q, inside, state, norm_gain.reshape(1, width))

    arrived = ctx_exchange(payload)

    half = out_weight.shape[1] // groups // 2
    holds = lambda n: [
        pltpu.VMEM((n, width, half), out_weight.dtype),
        pltpu.SemaphoreType.DMA((n,)),
    ]
    piece = jax.ShapeDtypeStruct((BAL * CH, half), jnp.bfloat16)
    packed, *across = pl.pallas_call(
        across_kernel,
        in_specs=[smem, vmem, hbm],
        out_specs=[vmem] * 3,
        out_shape=[jax.ShapeDtypeStruct((BAL * CH, width), jnp.bfloat16), piece, piece],
        scratch_shapes=[pltpu.VMEM((BAL * CH, width), jnp.float32), *holds(2)],
        compiler_params=params,
        name="across",
    )(slots, arrived, in_hbm(out_weight))
    beside = pl.pallas_call(
        beside_kernel,
        in_specs=[vmem, hbm],
        out_specs=[vmem] * 4,
        out_shape=[piece] * 4,
        scratch_shapes=holds(4),
        compiler_params=params,
        name="beside",
    )(packed, in_hbm(out_weight))
    own = pl.pallas_call(
        own_kernel,
        in_specs=[vmem, hbm],
        out_specs=[vmem] * 2,
        out_shape=[piece] * 2,
        scratch_shapes=holds(2),
        compiler_params=params,
        name="own",
    )(packed, in_hbm(out_weight))
    across, ahead, behind = across, beside[:2], beside[2:]
    return reduce_heads(across, ahead, behind, own)


def solution(mesh):
    placed = (
        P("ctx", "head"),
        P("ctx", "head"),
        P("ctx", "head"),
        P("head", None),
        P("head"),
        P(),
        P("ctx"),
        P("ctx"),
        P(),
    )
    return jax.shard_map(
        per_device, mesh=mesh, in_specs=placed, out_specs=P("ctx", "head"), check_vma=False
    )
```

```python
import jax
import jax.numpy as jnp
from jax import lax
from jax.experimental import pallas as pl
from jax.experimental.pallas import tpu as pltpu
from jax.sharding import PartitionSpec as P

DH = 128
CH = 8
BAL = 32
SESSIONS = 4
EPSILON = 1e-06
FAR = 1 << 28
SMEM = pltpu.MemorySpace.SMEM
VMEM = pltpu.MemorySpace.VMEM
HBM = pltpu.MemorySpace.HBM


def feature(block):
    value = block.astype(jnp.float32)
    return jnp.where(value > 0, value + 1.0, jnp.exp(jnp.minimum(value, 0.0))).astype(jnp.bfloat16)


def entry_kernel(counts, starts, device, slot, keys_hbm, values_hbm, out, info, keys, values, done):
    ranks = counts.shape[0]
    here = lax.axis_index("ctx")
    rows, width = keys.shape
    part = width // ranks
    copies = []
    for h in range(width // DH):
        columns = slice(DH * h, DH * (h + 1))
        pair = [
            pltpu.make_async_copy(source.at[:, columns], held.at[:, columns], done.at[i, h])
            for i, (source, held) in enumerate(((keys_hbm, keys), (values_hbm, values)))
        ]
        copies.append(pair)
        for copy in pair:
            copy.start()

    def add(k, total):
        return total + jnp.where(k < here, counts[k], 0)

    offset = CH * lax.fori_loop(0, ranks, add, jnp.int32(0), unroll=8)
    live = CH * counts[here]
    last_start = jnp.int32(-FAR)
    next_start = jnp.int32(FAR)
    for b in range(SESSIONS):
        local = starts[b] - offset
        info[3 + b] = local
        last_start = jnp.maximum(last_start, jnp.where(local <= live - 1, local, -FAR))
        next_start = jnp.minimum(next_start, jnp.where(local >= 0, local, FAR))
    info[0] = last_start
    info[1] = live
    info[2] = next_start
    info[7] = counts[here]

    out[:, part:, :] = jnp.full((ranks, out.shape[1] - part, DH), -1.0, jnp.bfloat16)

    def mark(j, carry):
        value = jnp.full((out.shape[1] - part, DH), slot[j], jnp.int32)
        out[device[j], part:, :] = value.astype(jnp.float32).astype(jnp.bfloat16)
        return carry

    lax.fori_loop(0, counts[here], mark, 0)

    row = lax.broadcasted_iota(jnp.int32, (rows, DH), 0)
    kept = (row >= last_start) & (row < live)
    each = DH // part
    for h in range(width // DH):
        columns = slice(DH * h, DH * (h + 1))
        for copy in copies[h]:
            copy.wait()
        phi = jnp.where(kept, feature(keys[:, columns]).astype(jnp.float32), 0.0)
        state = lax.dot_general(
            phi.astype(jnp.bfloat16),
            values[:, columns],
            (((0,), (0,)), ((), ())),
            preferred_element_type=jnp.float32,
        ).astype(jnp.bfloat16)
        for i in range(each):
            out[each * h + i, :part, :] = state[part * i : part * (i + 1), :]


def prefix_kernel(counts, starts, got, out, slots, marks, done):
    ranks, part, _ = out.shape
    lane = lax.broadcasted_iota(jnp.int32, (8, DH), 1)
    gathered = jnp.zeros((8, DH), jnp.float32)
    for k in range(ranks):
        gathered = jnp.where(lane == k, got[k, part:, :].astype(jnp.float32), gathered)
    marks[...] = gathered[:1].astype(jnp.int32)
    copy = pltpu.make_async_copy(marks, slots, done)
    copy.start()
    running = jnp.zeros((part, DH), jnp.float32)
    first = jnp.int32(0)
    for k in range(ranks):
        out[k] = running.astype(jnp.bfloat16)
        after = first + CH * counts[k]
        reset = jnp.int32(0)
        for b in range(SESSIONS):
            reset = reset | ((starts[b] >= first) & (starts[b] < after)).astype(jnp.int32)
        first = after
        if k + 1 < ranks:
            keep = jnp.full((part, DH), 1 - reset, jnp.int32) > 0
            running = jnp.where(keep, running, 0.0) + got[k, :part, :].astype(jnp.float32)
    copy.wait()


def inside_kernel(info, queries, keys, values, phi_out, out):
    rows, width = queries.shape
    row = lax.broadcasted_iota(jnp.int32, (rows, 1), 0)
    lower = jnp.full((rows, 1), -FAR, jnp.int32)
    for b in range(SESSIONS):
        lower = jnp.maximum(lower, jnp.where(row >= info[3 + b], info[3 + b], -FAR))
    column = lax.broadcasted_iota(jnp.int32, (rows, rows), 1)
    allowed = (column <= row) & (column >= lower)
    for h in range(width // DH):
        columns = slice(DH * h, DH * (h + 1))
        phi_q = feature(queries[:, columns])
        phi_k = feature(keys[:, columns])
        phi_out[:, columns] = phi_q
        scores = lax.dot_general(
            phi_q, phi_k, (((1,), (1,)), ((), ())), preferred_element_type=jnp.float32
        )
        scores = jnp.where(allowed, scores, 0.0).astype(jnp.bfloat16)
        out[:, columns] = jnp.dot(
            scores, values[:, columns], preferred_element_type=jnp.float32
        ).astype(jnp.bfloat16)


def attend_kernel(info, device, phi_q, inside, state, gain, out, scratch):
    rows, width = phi_q.shape
    row = lax.broadcasted_iota(jnp.int32, (rows, 1), 0)
    open_row = row < info[2]
    for h in range(width // DH):
        columns = slice(DH * h, DH * (h + 1))
        carried = jnp.dot(phi_q[:, columns], state[h], preferred_element_type=jnp.float32)
        numer = inside[:, columns].astype(jnp.float32) + jnp.where(open_row, carried, 0.0)
        inverse = lax.rsqrt(jnp.mean(numer * numer, axis=1, keepdims=True) + EPSILON)
        scratch[:, columns] = numer * inverse * gain[:, columns]

    def place(j, carry):
        start = pl.multiple_of(j * CH, CH)
        out[device[j]] = scratch[pl.ds(start, CH), :].astype(jnp.bfloat16)
        return carry

    lax.fori_loop(0, info[7], place, 0)


def column_copies(weight, held, done, pieces):
    groups = lax.axis_size("head")
    block = weight.shape[1] // groups
    half = block // 2
    copies = []
    for n, (by, i) in enumerate(pieces):
        column = lax.rem(lax.axis_index("head") + by, groups)
        start = pl.multiple_of(column * block + i * half, half)
        copies.append(
            pltpu.make_async_copy(weight.at[:, pl.ds(start, half)], held.at[n], done.at[n])
        )
    for copy in copies:
        copy.start()
    return copies


def products(packed, held, copies, outs):
    for n, (copy, out) in enumerate(zip(copies, outs)):
        copy.wait()
        out[...] = jnp.dot(packed[...], held[n], preferred_element_type=jnp.float32).astype(
            jnp.bfloat16
        )


def across_kernel(slots, arrived, weight, packed, left, right, gathered, held, done):
    copies = column_copies(weight, held, done, ((2, 0), (2, 1)))
    for s in range(arrived.shape[0]):
        slot = slots[0, s]

        @pl.when(slot >= 0)
        def _():
            start = pl.multiple_of(slot * CH, CH)
            gathered[pl.ds(start, CH), :] = arrived[s].astype(jnp.float32)

    packed[...] = gathered[...].astype(jnp.bfloat16)
    products(packed, held, copies, (left, right))


def beside_kernel(packed, weight, ahead_right, behind_left, kept, held, done, kept_done):
    last = lax.axis_size("head") - 1
    copies = column_copies(weight, held, done, ((1, 1), (last, 0)))
    later = column_copies(weight, kept, kept_done, ((1, 0), (last, 1)))
    products(packed, held, copies, (ahead_right, behind_left))
    for copy in later:
        copy.wait()


def join_kernel(packed, kept, up, down, left, right):
    for n, (arrived, out) in enumerate(((up, left), (down, right))):
        own = jnp.dot(packed[...], kept[n], preferred_element_type=jnp.float32)
        own = own.astype(jnp.bfloat16).astype(jnp.float32)
        out[...] = (own + arrived[...].astype(jnp.float32)).astype(jnp.bfloat16)


def own_kernel(packed, weight, from_ahead, from_behind, left, right, held, done):
    copies = column_copies(weight, held, done, ((0, 0), (0, 1)))
    for n, (arrived, out) in enumerate(((from_ahead, left), (from_behind, right))):
        copies[n].wait()
        own = jnp.dot(packed[...], held[n], preferred_element_type=jnp.float32)
        own = own.astype(jnp.bfloat16).astype(jnp.float32)
        out[...] = own + arrived[...].astype(jnp.float32)


def ctx_exchange(x):
    return lax.all_to_all(x, "ctx", split_axis=0, concat_axis=0, tiled=True)


def head_shift(x, by):
    count = lax.axis_size("head")
    return lax.ppermute(x, "head", [(i, (i + by) % count) for i in range(count)])


def wide(x):
    return x.astype(jnp.float32)


def per_device(
    queries,
    keys,
    values,
    out_weight,
    norm_gain,
    tile_counts,
    route_device,
    route_slot,
    session_starts,
):
    ranks = lax.axis_size("ctx")
    groups = lax.axis_size("head")
    rows, width = queries.shape
    heads = width // DH
    part = heads * DH // ranks
    smem = pl.BlockSpec(memory_space=SMEM)
    vmem = pl.BlockSpec(memory_space=VMEM)
    hbm = pl.BlockSpec(memory_space=HBM)
    in_hbm = lambda x: pltpu.with_memory_space_constraint(x, HBM)
    params = pltpu.CompilerParams(vmem_limit_bytes=16 << 20)

    tile_counts, session_starts, route_device, route_slot = map(
        in_hbm, (tile_counts, session_starts, route_device, route_slot)
    )
    entry, info = pl.pallas_call(
        entry_kernel,
        in_specs=[smem] * 4 + [hbm] * 2,
        out_specs=[vmem, smem],
        out_shape=[
            jax.ShapeDtypeStruct((ranks, part + 8, DH), jnp.bfloat16),
            jax.ShapeDtypeStruct((8,), jnp.int32),
        ],
        scratch_shapes=[
            pltpu.VMEM((rows, width), keys.dtype),
            pltpu.VMEM((rows, width), values.dtype),
            pltpu.SemaphoreType.DMA((2, heads)),
        ],
        compiler_params=params,
        name="entry",
    )(tile_counts, session_starts, route_device, route_slot, in_hbm(keys), in_hbm(values))

    got = ctx_exchange(entry)

    phi_q, inside = pl.pallas_call(
        inside_kernel,
        in_specs=[smem] + [vmem] * 3,
        out_specs=[vmem] * 2,
        out_shape=[
            jax.ShapeDtypeStruct((rows, width), jnp.bfloat16),
            jax.ShapeDtypeStruct((rows, width), jnp.bfloat16),
        ],
        compiler_params=params,
        name="inside",
    )(info, queries, keys, values)

    got, phi_q, inside = lax.optimization_barrier((got, phi_q, inside))
    summed, slots = pl.pallas_call(
        prefix_kernel,
        in_specs=[smem, smem, vmem],
        out_specs=[vmem, smem],
        out_shape=[
            jax.ShapeDtypeStruct((ranks, part, DH), jnp.bfloat16),
            jax.ShapeDtypeStruct((1, DH), jnp.int32),
        ],
        scratch_shapes=[pltpu.VMEM((1, DH), jnp.int32), pltpu.SemaphoreType.DMA],
        compiler_params=params,
        name="prefix",
    )(tile_counts, session_starts, got)

    state = ctx_exchange(summed).reshape(heads, DH, DH)

    payload = pl.pallas_call(
        attend_kernel,
        in_specs=[smem] * 2 + [vmem] * 4,
        out_specs=vmem,
        out_shape=jax.ShapeDtypeStruct((ranks, CH, width), jnp.bfloat16),
        scratch_shapes=[pltpu.VMEM((rows, width), jnp.float32)],
        compiler_params=params,
        name="attend",
    )(info, route_device, phi_q, inside, state, in_hbm(norm_gain.reshape(1, width)))

    arrived = ctx_exchange(payload)

    half = out_weight.shape[1] // groups // 2
    holds = lambda n: [
        pltpu.VMEM((n, width, half), out_weight.dtype),
        pltpu.SemaphoreType.DMA((n,)),
    ]
    piece = jax.ShapeDtypeStruct((BAL * CH, half), jnp.bfloat16)
    packed, *across = pl.pallas_call(
        across_kernel,
        in_specs=[smem, vmem, hbm],
        out_specs=[vmem] * 3,
        out_shape=[jax.ShapeDtypeStruct((BAL * CH, width), jnp.bfloat16), piece, piece],
        scratch_shapes=[pltpu.VMEM((BAL * CH, width), jnp.float32), *holds(2)],
        compiler_params=params,
        name="across",
    )(slots, arrived, in_hbm(out_weight))
    up = head_shift(across[0], 1)
    down = head_shift(across[1], -1)

    ahead_right, behind_left, kept = pl.pallas_call(
        beside_kernel,
        in_specs=[vmem, hbm],
        out_specs=[vmem] * 3,
        out_shape=[piece] * 2 + [jax.ShapeDtypeStruct((2, width, half), out_weight.dtype)],
        scratch_shapes=holds(2) + [pltpu.SemaphoreType.DMA((2,))],
        compiler_params=params,
        name="beside",
    )(packed, in_hbm(out_weight))
    from_behind = head_shift(ahead_right, 1)
    from_ahead = head_shift(behind_left, -1)

    left_sum, right_sum = pl.pallas_call(
        join_kernel,
        in_specs=[vmem] * 4,
        out_specs=[vmem] * 2,
        out_shape=[piece] * 2,
        compiler_params=params,
        name="join",
    )(packed, kept, up, down)
    last_left = head_shift(left_sum, 1)
    last_right = head_shift(right_sum, -1)

    left, right = pl.pallas_call(
        own_kernel,
        in_specs=[vmem, hbm, vmem, vmem],
        out_specs=[vmem] * 2,
        out_shape=[jax.ShapeDtypeStruct((BAL * CH, half), jnp.float32)] * 2,
        scratch_shapes=holds(2),
        compiler_params=params,
        name="own",
    )(packed, in_hbm(out_weight), from_ahead, from_behind)
    left = left + wide(last_left)
    right = right + wide(last_right)
    return jnp.concatenate([left, right], axis=1).astype(jnp.bfloat16)


def solution(mesh):
    placed = (
        P("ctx", "head"),
        P("ctx", "head"),
        P("ctx", "head"),
        P("head", None),
        P("head"),
        P(),
        P("ctx"),
        P("ctx"),
        P(),
    )
    return jax.shard_map(
        per_device, mesh=mesh, in_specs=placed, out_specs=P("ctx", "head"), check_vma=False
    )
```

```python
import jax
import jax.numpy as jnp
from jax import lax
from jax.experimental import pallas as pl
from jax.experimental.pallas import tpu as pltpu
from jax.sharding import PartitionSpec as P

DH = 128
CH = 8
BAL = 32
SESSIONS = 4
EPSILON = 1e-06
FAR = 1 << 28
SMEM = pltpu.MemorySpace.SMEM
VMEM = pltpu.MemorySpace.VMEM
HBM = pltpu.MemorySpace.HBM


def feature(block):
    value = block.astype(jnp.float32)
    return jnp.where(value > 0, value + 1.0, jnp.exp(jnp.minimum(value, 0.0))).astype(jnp.bfloat16)


def entry_kernel(counts, starts, keys_hbm, values_hbm, out, info, keys, values, done):
    ranks = counts.shape[0]
    here = lax.axis_index("ctx")
    rows, width = keys.shape
    part = width // ranks
    copies = []
    for h in range(width // DH):
        columns = slice(DH * h, DH * (h + 1))
        pair = [
            pltpu.make_async_copy(source.at[:, columns], held.at[:, columns], done.at[i, h])
            for i, (source, held) in enumerate(((keys_hbm, keys), (values_hbm, values)))
        ]
        copies.append(pair)
        for copy in pair:
            copy.start()

    def add(k, total):
        return total + jnp.where(k < here, counts[k], 0)

    offset = CH * lax.fori_loop(0, ranks, add, jnp.int32(0), unroll=8)
    live = CH * counts[here]
    last_start = jnp.int32(-FAR)
    next_start = jnp.int32(FAR)
    for b in range(SESSIONS):
        local = starts[b] - offset
        info[3 + b] = local
        last_start = jnp.maximum(last_start, jnp.where(local <= live - 1, local, -FAR))
        next_start = jnp.minimum(next_start, jnp.where(local >= 0, local, FAR))
    info[0] = last_start
    info[1] = live
    info[2] = next_start
    info[7] = counts[here]

    row = lax.broadcasted_iota(jnp.int32, (rows, DH), 0)
    kept = (row >= last_start) & (row < live)
    each = DH // part
    for h in range(width // DH):
        columns = slice(DH * h, DH * (h + 1))
        for copy in copies[h]:
            copy.wait()
        phi = jnp.where(kept, feature(keys[:, columns]).astype(jnp.float32), 0.0)
        state = lax.dot_general(
            phi.astype(jnp.bfloat16),
            values[:, columns],
            (((0,), (0,)), ((), ())),
            preferred_element_type=jnp.float32,
        ).astype(jnp.bfloat16)
        for i in range(each):
            out[each * h + i] = state[part * i : part * (i + 1), :]


def prefix_kernel(counts, starts, got, marks, out):
    ranks, part, _ = got.shape
    running = jnp.zeros((part, DH), jnp.float32)
    first = jnp.int32(0)
    for k in range(ranks):
        out[k, :part, :] = running.astype(jnp.bfloat16)
        out[k, part:, :] = marks[k]
        after = first + CH * counts[k]
        reset = jnp.int32(0)
        for b in range(SESSIONS):
            reset = reset | ((starts[b] >= first) & (starts[b] < after)).astype(jnp.int32)
        first = after
        if k + 1 < ranks:
            keep = jnp.full((part, DH), 1 - reset, jnp.int32) > 0
            running = jnp.where(keep, running, 0.0) + got[k].astype(jnp.float32)


def inside_kernel(info, device, slot, queries, keys, values, phi_out, out, marks):
    marks[...] = jnp.full(marks.shape, -1.0, marks.dtype)

    def mark(j, carry):
        value = jnp.full(marks.shape[1:], slot[j], jnp.int32)
        marks[device[j]] = value.astype(jnp.float32).astype(marks.dtype)
        return carry

    lax.fori_loop(0, info[7], mark, 0)
    rows, width = queries.shape
    row = lax.broadcasted_iota(jnp.int32, (rows, 1), 0)
    lower = jnp.full((rows, 1), -FAR, jnp.int32)
    for b in range(SESSIONS):
        lower = jnp.maximum(lower, jnp.where(row >= info[3 + b], info[3 + b], -FAR))
    column = lax.broadcasted_iota(jnp.int32, (rows, rows), 1)
    allowed = (column <= row) & (column >= lower)
    for h in range(width // DH):
        columns = slice(DH * h, DH * (h + 1))
        phi_q = feature(queries[:, columns])
        phi_k = feature(keys[:, columns])
        phi_out[:, columns] = phi_q
        scores = lax.dot_general(
            phi_q, phi_k, (((1,), (1,)), ((), ())), preferred_element_type=jnp.float32
        )
        scores = jnp.where(allowed, scores, 0.0).astype(jnp.bfloat16)
        out[:, columns] = jnp.dot(
            scores, values[:, columns], preferred_element_type=jnp.float32
        ).astype(jnp.bfloat16)


def attend_kernel(info, device, phi_q, inside, state, gain, out, slots, scratch, marks, done):
    rows, width = phi_q.shape
    ranks, part, _ = state.shape
    part = part - CH
    each = DH // part
    lane = lax.broadcasted_iota(jnp.int32, (CH, DH), 1)
    gathered = jnp.zeros((CH, DH), jnp.float32)
    for k in range(ranks):
        gathered = jnp.where(lane == k, state[k, part:, :].astype(jnp.float32), gathered)
    marks[...] = gathered[:1].astype(jnp.int32)
    copy = pltpu.make_async_copy(marks, slots, done)
    copy.start()
    row = lax.broadcasted_iota(jnp.int32, (rows, 1), 0)
    open_row = row < info[2]
    for h in range(width // DH):
        columns = slice(DH * h, DH * (h + 1))
        entered = jnp.concatenate([state[each * h + i, :part, :] for i in range(each)], axis=0)
        carried = jnp.dot(phi_q[:, columns], entered, preferred_element_type=jnp.float32)
        numer = inside[:, columns].astype(jnp.float32) + jnp.where(open_row, carried, 0.0)
        inverse = lax.rsqrt(jnp.mean(numer * numer, axis=1, keepdims=True) + EPSILON)
        scratch[:, columns] = numer * inverse * gain[:, columns]

    def place(j, carry):
        start = pl.multiple_of(j * CH, CH)
        out[device[j]] = scratch[pl.ds(start, CH), :].astype(jnp.bfloat16)
        return carry

    lax.fori_loop(0, info[7], place, 0)
    copy.wait()


def column_copies(weight, held, done, pieces):
    groups = lax.axis_size("head")
    block = weight.shape[1] // groups
    half = block // 2
    copies = []
    for n, (by, i) in enumerate(pieces):
        column = lax.rem(lax.axis_index("head") + by, groups)
        start = pl.multiple_of(column * block + i * half, half)
        copies.append(
            pltpu.make_async_copy(weight.at[:, pl.ds(start, half)], held.at[n], done.at[n])
        )
    for copy in copies:
        copy.start()
    return copies


def products(packed, held, copies, outs):
    for n, (copy, out) in enumerate(zip(copies, outs)):
        copy.wait()
        out[...] = jnp.dot(packed[...], held[n], preferred_element_type=jnp.float32).astype(
            jnp.bfloat16
        )


def across_kernel(slots, arrived, weight, packed, left, right, kept, source, held, done, later):
    last = lax.axis_size("head") - 1
    copies = column_copies(weight, held, done, ((2, 0), (2, 1)))
    pieces = ((1, 1), (last, 0), (1, 0), (last, 1), (0, 0), (0, 1))
    rest = column_copies(weight, kept, later, pieces)
    for s in range(arrived.shape[0]):
        slot = slots[0, s]
        source[jnp.where(slot < 0, BAL, slot)] = jnp.int32(s)
    for i in range(0, BAL, 2):
        packed[CH * i : CH * (i + 2), :] = jnp.concatenate(
            [arrived[source[i]], arrived[source[i + 1]]], axis=0
        )
    products(packed, held, copies, (left, right))
    for copy in rest:
        copy.wait()


def beside_kernel(packed, kept, ahead_right, behind_left):
    for n, out in enumerate((ahead_right, behind_left)):
        out[...] = jnp.dot(packed[...], kept[n], preferred_element_type=jnp.float32).astype(
            jnp.bfloat16
        )


def join_kernel(packed, kept, up, down, left, right):
    for n, (arrived, out) in enumerate(((up, left), (down, right))):
        own = jnp.dot(packed[...], kept[2 + n], preferred_element_type=jnp.float32)
        own = own.astype(jnp.bfloat16).astype(jnp.float32)
        out[...] = (own + arrived[...].astype(jnp.float32)).astype(jnp.bfloat16)


def own_kernel(packed, kept, from_ahead, from_behind, left, right):
    for n, (arrived, out) in enumerate(((from_ahead, left), (from_behind, right))):
        own = jnp.dot(packed[...], kept[4 + n], preferred_element_type=jnp.float32)
        own = own.astype(jnp.bfloat16).astype(jnp.float32)
        out[...] = own + arrived[...].astype(jnp.float32)


def ctx_exchange(x):
    return lax.all_to_all(x, "ctx", split_axis=0, concat_axis=0, tiled=True)


def head_shift(x, by):
    count = lax.axis_size("head")
    return lax.ppermute(x, "head", [(i, (i + by) % count) for i in range(count)])


def wide(x):
    return x.astype(jnp.float32)


def per_device(
    queries,
    keys,
    values,
    out_weight,
    norm_gain,
    tile_counts,
    route_device,
    route_slot,
    session_starts,
):
    ranks = lax.axis_size("ctx")
    groups = lax.axis_size("head")
    rows, width = queries.shape
    heads = width // DH
    part = heads * DH // ranks
    smem = pl.BlockSpec(memory_space=SMEM)
    vmem = pl.BlockSpec(memory_space=VMEM)
    hbm = pl.BlockSpec(memory_space=HBM)
    in_hbm = lambda x: pltpu.with_memory_space_constraint(x, HBM)
    params = pltpu.CompilerParams(vmem_limit_bytes=16 << 20)

    tile_counts, session_starts, route_device, route_slot = map(
        in_hbm, (tile_counts, session_starts, route_device, route_slot)
    )
    entry, info = pl.pallas_call(
        entry_kernel,
        in_specs=[smem] * 2 + [hbm] * 2,
        out_specs=[vmem, smem],
        out_shape=[
            jax.ShapeDtypeStruct((ranks, part, DH), jnp.bfloat16),
            jax.ShapeDtypeStruct((8,), jnp.int32),
        ],
        scratch_shapes=[
            pltpu.VMEM((rows, width), keys.dtype),
            pltpu.VMEM((rows, width), values.dtype),
            pltpu.SemaphoreType.DMA((2, heads)),
        ],
        compiler_params=params,
        name="entry",
    )(tile_counts, session_starts, in_hbm(keys), in_hbm(values))

    got = ctx_exchange(entry)

    phi_q, inside, marks = pl.pallas_call(
        inside_kernel,
        in_specs=[smem] * 3 + [vmem] * 3,
        out_specs=[vmem] * 3,
        out_shape=[
            jax.ShapeDtypeStruct((rows, width), jnp.bfloat16),
            jax.ShapeDtypeStruct((rows, width), jnp.bfloat16),
            jax.ShapeDtypeStruct((ranks, CH, DH), jnp.bfloat16),
        ],
        compiler_params=params,
        name="inside",
    )(info, route_device, route_slot, queries, keys, values)

    got, phi_q, inside, marks = lax.optimization_barrier((got, phi_q, inside, marks))
    summed = pl.pallas_call(
        prefix_kernel,
        in_specs=[smem, smem, vmem, vmem],
        out_specs=vmem,
        out_shape=jax.ShapeDtypeStruct((ranks, part + CH, DH), jnp.bfloat16),
        compiler_params=params,
        name="prefix",
    )(tile_counts, session_starts, got, marks)

    state = ctx_exchange(summed)

    payload, slots = pl.pallas_call(
        attend_kernel,
        in_specs=[smem] * 2 + [vmem] * 4,
        out_specs=[vmem, smem],
        out_shape=[
            jax.ShapeDtypeStruct((ranks, CH, width), jnp.bfloat16),
            jax.ShapeDtypeStruct((1, DH), jnp.int32),
        ],
        scratch_shapes=[
            pltpu.VMEM((rows, width), jnp.float32),
            pltpu.VMEM((1, DH), jnp.int32),
            pltpu.SemaphoreType.DMA,
        ],
        compiler_params=params,
        name="attend",
    )(info, route_device, phi_q, inside, state, in_hbm(norm_gain.reshape(1, width)))

    arrived = ctx_exchange(payload)

    half = out_weight.shape[1] // groups // 2
    piece = jax.ShapeDtypeStruct((BAL * CH, half), jnp.bfloat16)
    packed, *across, kept = pl.pallas_call(
        across_kernel,
        in_specs=[smem, vmem, hbm],
        out_specs=[vmem] * 4,
        out_shape=[
            jax.ShapeDtypeStruct((BAL * CH, width), jnp.bfloat16),
            piece,
            piece,
            jax.ShapeDtypeStruct((6, width, half), out_weight.dtype),
        ],
        scratch_shapes=[
            pltpu.SMEM((BAL + 1,), jnp.int32),
            pltpu.VMEM((2, width, half), out_weight.dtype),
            pltpu.SemaphoreType.DMA((2,)),
            pltpu.SemaphoreType.DMA((6,)),
        ],
        compiler_params=params,
        name="across",
    )(slots, arrived, in_hbm(out_weight))
    up = head_shift(across[0], 1)
    down = head_shift(across[1], -1)

    ahead_right, behind_left = pl.pallas_call(
        beside_kernel,
        in_specs=[vmem] * 2,
        out_specs=[vmem] * 2,
        out_shape=[piece] * 2,
        compiler_params=params,
        name="beside",
    )(packed, kept)
    from_behind = head_shift(ahead_right, 1)
    from_ahead = head_shift(behind_left, -1)

    left_sum, right_sum = pl.pallas_call(
        join_kernel,
        in_specs=[vmem] * 4,
        out_specs=[vmem] * 2,
        out_shape=[piece] * 2,
        compiler_params=params,
        name="join",
    )(packed, kept, up, down)
    last_left = head_shift(left_sum, 1)
    last_right = head_shift(right_sum, -1)

    left, right = pl.pallas_call(
        own_kernel,
        in_specs=[vmem] * 4,
        out_specs=[vmem] * 2,
        out_shape=[jax.ShapeDtypeStruct((BAL * CH, half), jnp.float32)] * 2,
        compiler_params=params,
        name="own",
    )(packed, kept, from_ahead, from_behind)
    left = left + wide(last_left)
    right = right + wide(last_right)
    return jnp.concatenate([left, right], axis=1).astype(jnp.bfloat16)


def solution(mesh):
    placed = (
        P("ctx", "head"),
        P("ctx", "head"),
        P("ctx", "head"),
        P("head", None),
        P("head"),
        P(),
        P("ctx"),
        P("ctx"),
        P(),
    )
    return jax.shard_map(
        per_device, mesh=mesh, in_specs=placed, out_specs=P("ctx", "head"), check_vma=False
    )
```

```python
import jax
import jax.numpy as jnp
from jax import lax
from jax.experimental import pallas as pl
from jax.experimental.pallas import tpu as pltpu
from jax.sharding import PartitionSpec as P

DH = 128
CH = 8
BAL = 32
SESSIONS = 4
GROUPS = 2
EPSILON = 1e-06
FAR = 1 << 28
SMEM = pltpu.MemorySpace.SMEM
VMEM = pltpu.MemorySpace.VMEM
HBM = pltpu.MemorySpace.HBM


def feature(block):
    value = block.astype(jnp.float32)
    return jnp.where(value > 0, value + 1.0, jnp.exp(jnp.minimum(value, 0.0))).astype(jnp.bfloat16)


def entry_kernel(
    counts_hbm, starts_hbm, device_hbm, slot_hbm, keys_hbm, values_hbm,
    out, info, keys, values, counts, starts, device, slot, done, small,
):
    ranks = counts.shape[0]
    here = lax.axis_index("ctx")
    rows, width = keys.shape
    part = width // ranks
    tables = ((counts_hbm, counts), (starts_hbm, starts), (device_hbm, device), (slot_hbm, slot))
    tables = [pltpu.make_async_copy(a, b, small.at[i]) for i, (a, b) in enumerate(tables)]
    for copy in tables:
        copy.start()
    copies = []
    for h in range(GROUPS):
        columns = slice(width // GROUPS * h, width // GROUPS * (h + 1))
        pair = [
            pltpu.make_async_copy(source.at[:, columns], held.at[:, columns], done.at[i, h])
            for i, (source, held) in enumerate(((keys_hbm, keys), (values_hbm, values)))
        ]
        copies.append(pair)
        for copy in pair:
            copy.start()
    for copy in tables:
        copy.wait()

    def add(k, total):
        return total + jnp.where(k < here, counts[k], 0)

    offset = CH * lax.fori_loop(0, ranks, add, jnp.int32(0), unroll=8)
    live = CH * counts[here]
    last_start = jnp.int32(-FAR)
    next_start = jnp.int32(FAR)
    for b in range(SESSIONS):
        local = starts[b] - offset
        info[3 + b] = local
        last_start = jnp.maximum(last_start, jnp.where(local <= live - 1, local, -FAR))
        next_start = jnp.minimum(next_start, jnp.where(local >= 0, local, FAR))
    info[0] = last_start
    info[1] = live
    info[2] = next_start
    info[7] = counts[here]

    out[:, part:, :] = jnp.full((ranks, CH, DH), -1.0, jnp.bfloat16)

    def mark(j, carry):
        value = jnp.full((CH, DH), slot[j], jnp.int32)
        out[device[j], part:, :] = value.astype(jnp.float32).astype(jnp.bfloat16)
        return carry

    lax.fori_loop(0, counts[here], mark, 0)

    row = lax.broadcasted_iota(jnp.int32, (rows, DH), 0)
    kept = (row >= last_start) & (row < live)
    each = DH // part
    for h in range(width // DH):
        columns = slice(DH * h, DH * (h + 1))
        if h % (width // DH // GROUPS) == 0:
            for copy in copies[h // (width // DH // GROUPS)]:
                copy.wait()
        phi = jnp.where(kept, feature(keys[:, columns]).astype(jnp.float32), 0.0)
        state = lax.dot_general(
            phi.astype(jnp.bfloat16),
            values[:, columns],
            (((0,), (0,)), ((), ())),
            preferred_element_type=jnp.float32,
        ).astype(jnp.bfloat16)
        for i in range(each):
            out[each * h + i, :part, :] = state[part * i : part * (i + 1), :]


def prefix_kernel(counts, starts, got, out, slots, marks, done):
    ranks, part, _ = out.shape
    lane = lax.broadcasted_iota(jnp.int32, (8, DH), 1)
    gathered = jnp.zeros((8, DH), jnp.float32)
    for k in range(ranks):
        gathered = jnp.where(lane == k, got[k, part:, :].astype(jnp.float32), gathered)
    marks[...] = gathered[:1].astype(jnp.int32)
    copy = pltpu.make_async_copy(marks, slots, done)
    copy.start()
    running = jnp.zeros((part, DH), jnp.float32)
    first = jnp.int32(0)
    for k in range(ranks):
        out[k] = running.astype(jnp.bfloat16)
        after = first + CH * counts[k]
        reset = jnp.int32(0)
        for b in range(SESSIONS):
            reset = reset | ((starts[b] >= first) & (starts[b] < after)).astype(jnp.int32)
        first = after
        if k + 1 < ranks:
            keep = jnp.full((part, DH), 1 - reset, jnp.int32) > 0
            running = jnp.where(keep, running, 0.0) + got[k, :part, :].astype(jnp.float32)
    copy.wait()


def column_copies(weight, held, done, pieces):
    groups = lax.axis_size("head")
    block = weight.shape[1] // groups
    half = block // 2
    copies = []
    for n, (by, i) in enumerate(pieces):
        column = lax.rem(lax.axis_index("head") + by, groups)
        start = pl.multiple_of(column * block + i * half, half)
        copies.append(
            pltpu.make_async_copy(weight.at[:, pl.ds(start, half)], held.at[n], done.at[n])
        )
    for copy in copies:
        copy.start()
    return copies


def inside_kernel(info, queries, keys, values, phi_out, out):
    rows, width = queries.shape
    row = lax.broadcasted_iota(jnp.int32, (rows, 1), 0)
    lower = jnp.full((rows, 1), -FAR, jnp.int32)
    for b in range(SESSIONS):
        lower = jnp.maximum(lower, jnp.where(row >= info[3 + b], info[3 + b], -FAR))
    column = lax.broadcasted_iota(jnp.int32, (rows, rows), 1)
    allowed = (column <= row) & (column >= lower)
    for h in range(width // DH):
        columns = slice(DH * h, DH * (h + 1))
        phi_q = feature(queries[:, columns])
        phi_k = feature(keys[:, columns])
        phi_out[:, columns] = phi_q
        scores = lax.dot_general(
            phi_q, phi_k, (((1,), (1,)), ((), ())), preferred_element_type=jnp.float32
        )
        scores = jnp.where(allowed, scores, 0.0).astype(jnp.bfloat16)
        out[:, columns] = jnp.dot(
            scores, values[:, columns], preferred_element_type=jnp.float32
        ).astype(jnp.bfloat16)


def attend_kernel(info, device, phi_q, inside, state, gain, weight, out, kept, scratch, done):
    last = lax.axis_size("head") - 1
    copies = column_copies(weight, kept, done, ((2, 0), (2, 1), (1, 1), (last, 0)))
    rows, width = phi_q.shape
    row = lax.broadcasted_iota(jnp.int32, (rows, 1), 0)
    open_row = row < info[2]
    for h in range(width // DH):
        columns = slice(DH * h, DH * (h + 1))
        carried = jnp.dot(phi_q[:, columns], state[h], preferred_element_type=jnp.float32)
        numer = inside[:, columns].astype(jnp.float32) + jnp.where(open_row, carried, 0.0)
        inverse = lax.rsqrt(jnp.mean(numer * numer, axis=1, keepdims=True) + EPSILON)
        scratch[:, columns] = numer * inverse * gain[:, columns]

    def place(j, carry):
        start = pl.multiple_of(j * CH, CH)
        out[device[j]] = scratch[pl.ds(start, CH), :].astype(jnp.bfloat16)
        return carry

    lax.fori_loop(0, info[7], place, 0)
    for copy in copies:
        copy.wait()


def products(packed, kept, first, outs):
    for n, out in enumerate(outs):
        out[...] = jnp.dot(
            packed[...], kept[first + n], preferred_element_type=jnp.float32
        ).astype(jnp.bfloat16)


def across_kernel(slots, arrived, kept, packed, left, right, source):
    for s in range(arrived.shape[0]):
        slot = slots[0, s]
        source[jnp.where(slot < 0, BAL, slot)] = jnp.int32(s)
    for i in range(0, BAL, 2):
        packed[CH * i : CH * (i + 2), :] = jnp.concatenate(
            [arrived[source[i]], arrived[source[i + 1]]], axis=0
        )
    products(packed, kept, 0, (left, right))


def beside_kernel(packed, early, weight, ahead_right, behind_left, later, done):
    last = lax.axis_size("head") - 1
    copies = column_copies(weight, later, done, ((1, 0), (last, 1), (0, 0), (0, 1)))
    products(packed, early, 2, (ahead_right, behind_left))
    for copy in copies:
        copy.wait()


def join_kernel(packed, kept, up, down, left, right):
    for n, (arrived, out) in enumerate(((up, left), (down, right))):
        own = jnp.dot(packed[...], kept[n], preferred_element_type=jnp.float32)
        own = own.astype(jnp.bfloat16).astype(jnp.float32)
        out[...] = (own + arrived[...].astype(jnp.float32)).astype(jnp.bfloat16)


def own_kernel(packed, kept, from_ahead, from_behind, left, right):
    for n, (arrived, out) in enumerate(((from_ahead, left), (from_behind, right))):
        own = jnp.dot(packed[...], kept[2 + n], preferred_element_type=jnp.float32)
        own = own.astype(jnp.bfloat16).astype(jnp.float32)
        out[...] = own + arrived[...].astype(jnp.float32)


def ctx_exchange(x):
    return lax.all_to_all(x, "ctx", split_axis=0, concat_axis=0, tiled=True)


def head_shift(x, by):
    count = lax.axis_size("head")
    return lax.ppermute(x, "head", [(i, (i + by) % count) for i in range(count)])


def wide(x):
    return x.astype(jnp.float32)


def per_device(
    queries,
    keys,
    values,
    out_weight,
    norm_gain,
    tile_counts,
    route_device,
    route_slot,
    session_starts,
):
    ranks = lax.axis_size("ctx")
    groups = lax.axis_size("head")
    rows, width = queries.shape
    heads = width // DH
    part = heads * DH // ranks
    smem = pl.BlockSpec(memory_space=SMEM)
    vmem = pl.BlockSpec(memory_space=VMEM)
    hbm = pl.BlockSpec(memory_space=HBM)
    in_hbm = lambda x: pltpu.with_memory_space_constraint(x, HBM)
    params = pltpu.CompilerParams(vmem_limit_bytes=16 << 20)

    tables = [in_hbm(x) for x in (tile_counts, session_starts, route_device, route_slot)]
    tile_counts, session_starts, route_device, route_slot = tables
    entry, info = pl.pallas_call(
        entry_kernel,
        in_specs=[hbm] * 6,
        out_specs=[vmem, smem],
        out_shape=[
            jax.ShapeDtypeStruct((ranks, part + CH, DH), jnp.bfloat16),
            jax.ShapeDtypeStruct((8,), jnp.int32),
        ],
        scratch_shapes=[
            pltpu.VMEM((rows, width), keys.dtype),
            pltpu.VMEM((rows, width), values.dtype),
            *[pltpu.SMEM(x.shape, jnp.int32) for x in tables],
            pltpu.SemaphoreType.DMA((2, GROUPS)),
            pltpu.SemaphoreType.DMA((4,)),
        ],
        compiler_params=params,
        name="entry",
    )(*tables, in_hbm(keys), in_hbm(values))

    got = ctx_exchange(entry)

    half = out_weight.shape[1] // groups // 2
    phi_q, inside = pl.pallas_call(
        inside_kernel,
        in_specs=[smem] + [vmem] * 3,
        out_specs=[vmem] * 2,
        out_shape=[jax.ShapeDtypeStruct((rows, width), jnp.bfloat16)] * 2,
        compiler_params=params,
        name="inside",
    )(info, queries, keys, values)

    got, phi_q, inside = lax.optimization_barrier((got, phi_q, inside))
    summed, slots = pl.pallas_call(
        prefix_kernel,
        in_specs=[smem, smem, vmem],
        out_specs=[vmem, smem],
        out_shape=[
            jax.ShapeDtypeStruct((ranks, part, DH), jnp.bfloat16),
            jax.ShapeDtypeStruct((1, DH), jnp.int32),
        ],
        scratch_shapes=[pltpu.VMEM((1, DH), jnp.int32), pltpu.SemaphoreType.DMA],
        compiler_params=params,
        name="prefix",
    )(tile_counts, session_starts, got)

    state = ctx_exchange(summed).reshape(heads, DH, DH)

    half = out_weight.shape[1] // groups // 2
    held = jax.ShapeDtypeStruct((4, width, half), out_weight.dtype)
    payload, early = pl.pallas_call(
        attend_kernel,
        in_specs=[smem] * 2 + [vmem] * 4 + [hbm],
        out_specs=[vmem] * 2,
        out_shape=[jax.ShapeDtypeStruct((ranks, CH, width), jnp.bfloat16), held],
        scratch_shapes=[pltpu.VMEM((rows, width), jnp.float32), pltpu.SemaphoreType.DMA((4,))],
        compiler_params=params,
        name="attend",
    )(
        info,
        route_device,
        phi_q,
        inside,
        state,
        in_hbm(norm_gain.reshape(1, width)),
        in_hbm(out_weight),
    )

    arrived = ctx_exchange(payload)

    piece = jax.ShapeDtypeStruct((BAL * CH, half), jnp.bfloat16)
    packed, *across = pl.pallas_call(
        across_kernel,
        in_specs=[smem, vmem, vmem],
        out_specs=[vmem] * 3,
        out_shape=[jax.ShapeDtypeStruct((BAL * CH, width), jnp.bfloat16), piece, piece],
        scratch_shapes=[pltpu.SMEM((BAL + 1,), jnp.int32)],
        compiler_params=params,
        name="across",
    )(slots, arrived, early)
    up = head_shift(across[0], 1)
    down = head_shift(across[1], -1)

    ahead_right, behind_left, later = pl.pallas_call(
        beside_kernel,
        in_specs=[vmem, vmem, hbm],
        out_specs=[vmem] * 3,
        out_shape=[piece, piece, held],
        scratch_shapes=[pltpu.SemaphoreType.DMA((4,))],
        compiler_params=params,
        name="beside",
    )(packed, early, in_hbm(out_weight))
    from_behind = head_shift(ahead_right, 1)
    from_ahead = head_shift(behind_left, -1)

    left_sum, right_sum = pl.pallas_call(
        join_kernel,
        in_specs=[vmem] * 4,
        out_specs=[vmem] * 2,
        out_shape=[piece] * 2,
        compiler_params=params,
        name="join",
    )(packed, later, up, down)
    last_left = head_shift(left_sum, 1)
    last_right = head_shift(right_sum, -1)

    left, right = pl.pallas_call(
        own_kernel,
        in_specs=[vmem] * 4,
        out_specs=[vmem] * 2,
        out_shape=[jax.ShapeDtypeStruct((BAL * CH, half), jnp.float32)] * 2,
        compiler_params=params,
        name="own",
    )(packed, later, from_ahead, from_behind)
    left = left + wide(last_left)
    right = right + wide(last_right)
    return jnp.concatenate([left, right], axis=1).astype(jnp.bfloat16)


def solution(mesh):
    placed = (
        P("ctx", "head"),
        P("ctx", "head"),
        P("ctx", "head"),
        P("head", None),
        P("head"),
        P(),
        P("ctx"),
        P("ctx"),
        P(),
    )
    return jax.shard_map(
        per_device, mesh=mesh, in_specs=placed, out_specs=P("ctx", "head"), check_vma=False
    )
```

```python
import jax
import jax.numpy as jnp
from jax import lax
from jax.experimental import pallas as pl
from jax.experimental.pallas import tpu as pltpu
from jax.sharding import PartitionSpec as P

DH = 128
CH = 8
BAL = 32
SESSIONS = 4
GROUPS = 2
EPSILON = 1e-06
FAR = 1 << 28
SMEM = pltpu.MemorySpace.SMEM
VMEM = pltpu.MemorySpace.VMEM
HBM = pltpu.MemorySpace.HBM


def feature(block):
    value = block.astype(jnp.float32)
    return jnp.where(value > 0, value + 1.0, jnp.exp(jnp.minimum(value, 0.0))).astype(jnp.bfloat16)


def entry_kernel(
    counts_hbm, starts_hbm, device_hbm, slot_hbm, keys_hbm, values_hbm,
    out, info, keys, values, counts, starts, device, slot, done, small,
):
    ranks = counts.shape[0]
    here = lax.axis_index("ctx")
    rows, width = keys.shape
    part = width // ranks
    tables = ((counts_hbm, counts), (starts_hbm, starts), (device_hbm, device), (slot_hbm, slot))
    tables = [pltpu.make_async_copy(a, b, small.at[i]) for i, (a, b) in enumerate(tables)]
    for copy in tables:
        copy.start()
    copies = []
    for h in range(GROUPS):
        columns = slice(width // GROUPS * h, width // GROUPS * (h + 1))
        pair = [
            pltpu.make_async_copy(source.at[:, columns], held.at[:, columns], done.at[i, h])
            for i, (source, held) in enumerate(((keys_hbm, keys), (values_hbm, values)))
        ]
        copies.append(pair)
        for copy in pair:
            copy.start()
    for copy in tables:
        copy.wait()

    def add(k, total):
        return total + jnp.where(k < here, counts[k], 0)

    offset = CH * lax.fori_loop(0, ranks, add, jnp.int32(0), unroll=8)
    live = CH * counts[here]
    last_start = jnp.int32(-FAR)
    next_start = jnp.int32(FAR)
    for b in range(SESSIONS):
        local = starts[b] - offset
        info[3 + b] = local
        last_start = jnp.maximum(last_start, jnp.where(local <= live - 1, local, -FAR))
        next_start = jnp.minimum(next_start, jnp.where(local >= 0, local, FAR))
    info[0] = last_start
    info[1] = live
    info[2] = next_start
    info[7] = counts[here]

    out[:, part:, :] = jnp.full((ranks, CH, DH), -1.0, jnp.bfloat16)

    def mark(j, carry):
        value = jnp.full((CH, DH), slot[j], jnp.int32)
        out[device[j], part:, :] = value.astype(jnp.float32).astype(jnp.bfloat16)
        return carry

    lax.fori_loop(0, counts[here], mark, 0)

    row = lax.broadcasted_iota(jnp.int32, (rows, DH), 0)
    kept = (row >= last_start) & (row < live)
    each = DH // part
    for h in range(width // DH):
        columns = slice(DH * h, DH * (h + 1))
        if h % (width // DH // GROUPS) == 0:
            for copy in copies[h // (width // DH // GROUPS)]:
                copy.wait()
        phi = jnp.where(kept, feature(keys[:, columns]).astype(jnp.float32), 0.0)
        state = lax.dot_general(
            phi.astype(jnp.bfloat16),
            values[:, columns],
            (((0,), (0,)), ((), ())),
            preferred_element_type=jnp.float32,
        ).astype(jnp.bfloat16)
        for i in range(each):
            out[each * h + i, :part, :] = state[part * i : part * (i + 1), :]


def prefix_kernel(counts, starts, got, out, slots, marks, done):
    ranks, part, _ = out.shape
    lane = lax.broadcasted_iota(jnp.int32, (8, DH), 1)
    gathered = jnp.zeros((8, DH), jnp.float32)
    for k in range(ranks):
        gathered = jnp.where(lane == k, got[k, part:, :].astype(jnp.float32), gathered)
    marks[...] = gathered[:1].astype(jnp.int32)
    copy = pltpu.make_async_copy(marks, slots, done)
    copy.start()
    running = jnp.zeros((part, DH), jnp.float32)
    first = jnp.int32(0)
    for k in range(ranks):
        out[k] = running.astype(jnp.bfloat16)
        after = first + CH * counts[k]
        reset = jnp.int32(0)
        for b in range(SESSIONS):
            reset = reset | ((starts[b] >= first) & (starts[b] < after)).astype(jnp.int32)
        first = after
        if k + 1 < ranks:
            keep = jnp.full((part, DH), 1 - reset, jnp.int32) > 0
            running = jnp.where(keep, running, 0.0) + got[k, :part, :].astype(jnp.float32)
    copy.wait()


def group_columns(width, h):
    return slice(width // GROUPS * h, width // GROUPS * (h + 1))


def inside_kernel(
    info, queries_hbm, keys_hbm, values_hbm, weight, phi_hbm, out_hbm, to_near, to_far,
    queries, keys, values, phi_out, out, done, cut_done, out_done,
):
    rows, width = queries.shape
    copies = []
    for h in range(GROUPS):
        columns = group_columns(width, h)
        pairs = ((queries_hbm, queries), (keys_hbm, keys), (values_hbm, values))
        copies.append(
            [
                pltpu.make_async_copy(source.at[:, columns], held.at[:, columns], done.at[i, h])
                for i, (source, held) in enumerate(pairs)
            ]
        )
        for copy in copies[h]:
            copy.start()
    cuts = cut_copies(weight, to_near, to_far, cut_done)
    for copy in cuts:
        copy.start()
    row = lax.broadcasted_iota(jnp.int32, (rows, 1), 0)
    lower = jnp.full((rows, 1), -FAR, jnp.int32)
    for b in range(SESSIONS):
        lower = jnp.maximum(lower, jnp.where(row >= info[3 + b], info[3 + b], -FAR))
    column = lax.broadcasted_iota(jnp.int32, (rows, rows), 1)
    allowed = (column <= row) & (column >= lower)
    leaving = []
    group = width // DH // GROUPS
    for h in range(width // DH):
        columns = slice(DH * h, DH * (h + 1))
        if h % group == 0:
            for copy in copies[h // group]:
                copy.wait()
        phi_q = feature(queries[:, columns])
        phi_k = feature(keys[:, columns])
        phi_out[:, columns] = phi_q
        scores = lax.dot_general(
            phi_q, phi_k, (((1,), (1,)), ((), ())), preferred_element_type=jnp.float32
        )
        scores = jnp.where(allowed, scores, 0.0).astype(jnp.bfloat16)
        out[:, columns] = jnp.dot(
            scores, values[:, columns], preferred_element_type=jnp.float32
        ).astype(jnp.bfloat16)
        if h % group == group - 1:
            ready = group_columns(width, h // group)
            for i, (held, target) in enumerate(((phi_out, phi_hbm), (out, out_hbm))):
                copy = pltpu.make_async_copy(
                    held.at[:, ready], target.at[:, ready], out_done.at[i, h // group]
                )
                copy.start()
                leaving.append(copy)
    for copy in leaving + cuts:
        copy.wait()


def attend_kernel(
    info, device, phi_hbm, inside_hbm, state, gain, out, scratch, phi_q, inside, done
):
    rows, width = phi_q.shape
    copies = []
    for h in range(GROUPS):
        columns = slice(width // GROUPS * h, width // GROUPS * (h + 1))
        pair = [
            pltpu.make_async_copy(source.at[:, columns], held.at[:, columns], done.at[i, h])
            for i, (source, held) in enumerate(((phi_hbm, phi_q), (inside_hbm, inside)))
        ]
        copies.append(pair)
        for copy in pair:
            copy.start()
    row = lax.broadcasted_iota(jnp.int32, (rows, 1), 0)
    open_row = row < info[2]
    for h in range(width // DH):
        columns = slice(DH * h, DH * (h + 1))
        if h % (width // DH // GROUPS) == 0:
            for copy in copies[h // (width // DH // GROUPS)]:
                copy.wait()
        carried = jnp.dot(phi_q[:, columns], state[h], preferred_element_type=jnp.float32)
        numer = inside[:, columns].astype(jnp.float32) + jnp.where(open_row, carried, 0.0)
        inverse = lax.rsqrt(jnp.mean(numer * numer, axis=1, keepdims=True) + EPSILON)
        scratch[:, columns] = numer * inverse * gain[:, columns]

    def place(j, carry):
        start = pl.multiple_of(j * CH, CH)
        out[device[j]] = scratch[pl.ds(start, CH), :].astype(jnp.bfloat16)
        return carry

    lax.fori_loop(0, info[7], place, 0)


def near(x):
    return x + 1 - 2 * lax.rem(x, 2)


def far(x):
    return lax.axis_size("head") - 1 - x


def cut_copies(weight, to_near, to_far, done):
    x = lax.axis_index("head")
    core = lax.rem(lax.axis_index("ctx"), 2)
    rows, block = to_near.shape[1:]
    top = pl.multiple_of(core * rows, rows)
    columns = (near(x), far(near(x)), far(x), near(far(x)))
    targets = (to_near.at[0], to_near.at[1], to_far.at[0], to_far.at[1])
    copies = []
    for n, (column, target) in enumerate(zip(columns, targets)):
        left = pl.multiple_of(column * block, block)
        copies.append(
            pltpu.make_async_copy(
                weight.at[pl.ds(top, rows), pl.ds(left, block)], target, done.at[n]
            )
        )
    return copies


def gather_kernel(slots, arrived, first, second, source):
    for s in range(arrived.shape[0]):
        slot = slots[0, s]
        source[jnp.where(slot < 0, BAL, slot)] = jnp.int32(s)
    for i in range(0, BAL, 2):
        out = first if i < BAL // 2 else second
        start = CH * (i % (BAL // 2))
        out[start : start + 2 * CH, :] = jnp.concatenate(
            [arrived[source[i]], arrived[source[i + 1]]], axis=0
        )


def own_kernel(
    first, second, weight, near_mine, near_other, far_mine, far_other,
    send_first, send_second, keep_first, keep_second, later, held, done, later_done,
):
    x = lax.axis_index("head")
    block = held.shape[2]
    copies = []
    for n, column in enumerate((far(x), near(x), x)):
        left = pl.multiple_of(column * block, block)
        copies.append(
            pltpu.make_async_copy(weight.at[:, pl.ds(left, block)], held.at[n], done.at[n])
        )
    rest = [
        pltpu.make_async_copy(piece.at[1], later.at[n], later_done.at[n])
        for n, piece in enumerate((near_mine, near_other, far_mine, far_other))
    ]
    for copy in copies + rest:
        copy.start()
    pairs = ((0, first, send_first), (1, second, send_second))
    for n, rows, out in pairs + ((2, first, keep_first), (2, second, keep_second)):
        if out is not keep_second:
            copies[n].wait()
        out[...] = jnp.dot(rows[...], held[n], preferred_element_type=jnp.float32)
    for copy in rest:
        copy.wait()


def both_halves(rows, mine, other):
    core = lax.rem(lax.axis_index("ctx"), 2)
    half = rows.shape[1] // 2
    total = None
    for place, weight in ((core, mine), (1 - core, other)):
        left = pl.multiple_of(place * half, half)
        part = jnp.dot(rows[:, pl.ds(left, half)], weight, preferred_element_type=jnp.float32)
        total = part if total is None else total + part
    return total


def join_kernel(from_near, from_far, later, send_first, send_second, out_first, out_second):
    total = send_first[...] + both_halves(from_near, later[0], later[1])
    out_first[...] = total.astype(jnp.bfloat16)
    total = send_second[...] + both_halves(from_far, later[2], later[3])
    out_second[...] = total.astype(jnp.bfloat16)


def keep_kernel(
    from_near, from_far, near_mine, near_other, far_mine, far_other,
    keep_first, keep_second, out_first, out_second, held, done,
):
    pieces = (near_mine, near_other, far_mine, far_other)
    copies = [
        pltpu.make_async_copy(piece.at[0], held.at[n], done.at[n])
        for n, piece in enumerate(pieces)
    ]
    for copy in copies:
        copy.start()
    copies[0].wait()
    copies[1].wait()
    out_first[...] = keep_first[...] + both_halves(from_near, held[0], held[1])
    copies[2].wait()
    copies[3].wait()
    out_second[...] = keep_second[...] + both_halves(from_far, held[2], held[3])


def ctx_exchange(x):
    return lax.all_to_all(x, "ctx", split_axis=0, concat_axis=0, tiled=True)


def near_swap(x):
    return lax.ppermute(x, "head", [(0, 1), (1, 0), (2, 3), (3, 2)])


def far_swap(x):
    return lax.ppermute(x, "head", [(0, 3), (3, 0), (1, 2), (2, 1)])


def core_swap(x):
    return lax.ppermute(x, "ctx", [(i, i ^ 1) for i in range(lax.axis_size("ctx"))])


def wide(x):
    return x.astype(jnp.float32)


def per_device(
    queries,
    keys,
    values,
    out_weight,
    norm_gain,
    tile_counts,
    route_device,
    route_slot,
    session_starts,
):
    ranks = lax.axis_size("ctx")
    groups = lax.axis_size("head")
    rows, width = queries.shape
    heads = width // DH
    part = heads * DH // ranks
    smem = pl.BlockSpec(memory_space=SMEM)
    vmem = pl.BlockSpec(memory_space=VMEM)
    hbm = pl.BlockSpec(memory_space=HBM)
    any_space = pl.BlockSpec(memory_space=pl.ANY)
    in_hbm = lambda x: pltpu.with_memory_space_constraint(x, HBM)
    params = pltpu.CompilerParams(vmem_limit_bytes=16 << 20)

    tables = [in_hbm(x) for x in (tile_counts, session_starts, route_device, route_slot)]
    tile_counts, session_starts, route_device, route_slot = tables
    entry, info = pl.pallas_call(
        entry_kernel,
        in_specs=[hbm] * 6,
        out_specs=[vmem, smem],
        out_shape=[
            jax.ShapeDtypeStruct((ranks, part + CH, DH), jnp.bfloat16),
            jax.ShapeDtypeStruct((8,), jnp.int32),
        ],
        scratch_shapes=[
            pltpu.VMEM((rows, width), keys.dtype),
            pltpu.VMEM((rows, width), values.dtype),
            *[pltpu.SMEM(x.shape, jnp.int32) for x in tables],
            pltpu.SemaphoreType.DMA((2, GROUPS)),
            pltpu.SemaphoreType.DMA((4,)),
        ],
        compiler_params=params,
        name="entry",
    )(*tables, in_hbm(keys), in_hbm(values))

    got = ctx_exchange(entry)

    block = out_weight.shape[1] // groups
    cut = HBM((2, width // 2, block), out_weight.dtype)
    local = HBM((rows, width), jnp.bfloat16)
    phi_q, inside, to_near, to_far = map(
        in_hbm,
        pl.pallas_call(
            inside_kernel,
            in_specs=[smem] + [hbm] * 4,
            out_specs=[hbm] * 4,
            out_shape=[local, local, cut, cut],
            scratch_shapes=[
                *[pltpu.VMEM((rows, width), jnp.bfloat16)] * 5,
                pltpu.SemaphoreType.DMA((3, GROUPS)),
                pltpu.SemaphoreType.DMA((4,)),
                pltpu.SemaphoreType.DMA((2, GROUPS)),
            ],
            compiler_params=params,
            name="inside",
        )(info, in_hbm(queries), in_hbm(keys), in_hbm(values), in_hbm(out_weight)),
    )

    got, phi_q, inside, to_near, to_far = lax.optimization_barrier(
        (got, phi_q, inside, to_near, to_far)
    )
    summed, slots = pl.pallas_call(
        prefix_kernel,
        in_specs=[smem, smem, vmem],
        out_specs=[vmem, smem],
        out_shape=[
            jax.ShapeDtypeStruct((ranks, part, DH), jnp.bfloat16),
            jax.ShapeDtypeStruct((1, DH), jnp.int32),
        ],
        scratch_shapes=[pltpu.VMEM((1, DH), jnp.int32), pltpu.SemaphoreType.DMA],
        compiler_params=params,
        name="prefix",
    )(tile_counts, session_starts, got)

    near_mine, far_mine = near_swap(to_near), far_swap(to_far)
    state = ctx_exchange(summed).reshape(heads, DH, DH)

    payload = pl.pallas_call(
        attend_kernel,
        in_specs=[smem] * 2 + [hbm] * 2 + [vmem] * 2,
        out_specs=vmem,
        out_shape=jax.ShapeDtypeStruct((ranks, CH, width), jnp.bfloat16),
        scratch_shapes=[
            pltpu.VMEM((rows, width), jnp.float32),
            pltpu.VMEM((rows, width), jnp.bfloat16),
            pltpu.VMEM((rows, width), jnp.bfloat16),
            pltpu.SemaphoreType.DMA((2, GROUPS)),
        ],
        compiler_params=params,
        name="attend",
    )(
        info,
        route_device,
        in_hbm(phi_q),
        in_hbm(inside),
        state,
        in_hbm(norm_gain.reshape(1, width)),
    )

    arrived = ctx_exchange(payload)

    near_mine, far_mine, _ = lax.optimization_barrier((near_mine, far_mine, payload))
    near_other, far_other = core_swap(near_mine), core_swap(far_mine)

    part_rows = BAL * CH // 2
    some = jax.ShapeDtypeStruct((part_rows, width), jnp.bfloat16)
    sent = jax.ShapeDtypeStruct((part_rows, block), jnp.bfloat16)
    exact = jax.ShapeDtypeStruct((part_rows, block), jnp.float32)
    first, second = pl.pallas_call(
        gather_kernel,
        in_specs=[smem, vmem],
        out_specs=[vmem] * 2,
        out_shape=[some] * 2,
        scratch_shapes=[pltpu.SMEM((BAL + 1,), jnp.int32)],
        compiler_params=params,
        name="gather",
    )(slots, arrived)
    from_near, from_far = near_swap(first), far_swap(second)

    weights = [in_hbm(near_mine), near_other, in_hbm(far_mine), far_other]
    *sums, later = pl.pallas_call(
        own_kernel,
        in_specs=[vmem] * 2 + [hbm] * 2 + [any_space, hbm, any_space],
        out_specs=[vmem] * 5,
        out_shape=[exact] * 4 + [jax.ShapeDtypeStruct((4, width // 2, block), out_weight.dtype)],
        scratch_shapes=[
            pltpu.VMEM((3, width, block), out_weight.dtype),
            pltpu.SemaphoreType.DMA((3,)),
            pltpu.SemaphoreType.DMA((4,)),
        ],
        compiler_params=params,
        name="own",
    )(first, second, in_hbm(out_weight), *weights)

    join_first, join_second = pl.pallas_call(
        join_kernel,
        in_specs=[vmem] * 5,
        out_specs=[vmem] * 2,
        out_shape=[sent] * 2,
        compiler_params=params,
        name="join",
    )(from_near, from_far, later, *sums[:2])
    last_first, last_second = far_swap(join_first), near_swap(join_second)

    keep_first, keep_second = pl.pallas_call(
        keep_kernel,
        in_specs=[vmem] * 2 + [hbm, any_space] * 2 + [vmem] * 2,
        out_specs=[vmem] * 2,
        out_shape=[exact] * 2,
        scratch_shapes=[
            pltpu.VMEM((4, width // 2, block), out_weight.dtype),
            pltpu.SemaphoreType.DMA((4,)),
        ],
        compiler_params=params,
        name="keep",
    )(from_near, from_far, *weights, *sums[2:])
    keep_first = keep_first + wide(last_first)
    keep_second = keep_second + wide(last_second)
    return jnp.concatenate([keep_first, keep_second], axis=0).astype(jnp.bfloat16)


def solution(mesh):
    placed = (
        P("ctx", "head"),
        P("ctx", "head"),
        P("ctx", "head"),
        P("head", None),
        P("head"),
        P(),
        P("ctx"),
        P("ctx"),
        P(),
    )
    return jax.shard_map(
        per_device, mesh=mesh, in_specs=placed, out_specs=P("ctx", "head"), check_vma=False
    )
```

```python
import jax
import jax.numpy as jnp
from jax import lax
from jax.experimental import pallas as pl
from jax.experimental.pallas import tpu as pltpu
from jax.sharding import PartitionSpec as P

DH = 128
CH = 8
BAL = 32
SESSIONS = 4
GROUPS = 2
EPSILON = 1e-06
FAR = 1 << 28
SMEM = pltpu.MemorySpace.SMEM
VMEM = pltpu.MemorySpace.VMEM
HBM = pltpu.MemorySpace.HBM


def feature(block):
    value = block.astype(jnp.float32)
    return jnp.where(value > 0, value + 1.0, jnp.exp(jnp.minimum(value, 0.0))).astype(jnp.bfloat16)


def entry_kernel(
    counts_hbm, starts_hbm, device_hbm, slot_hbm, keys_hbm, values_hbm,
    out, info, keys, values, counts, starts, device, slot, done, small,
):
    ranks = counts.shape[0]
    here = lax.axis_index("ctx")
    rows, width = keys.shape
    part = width // ranks
    tables = ((counts_hbm, counts), (starts_hbm, starts), (device_hbm, device), (slot_hbm, slot))
    tables = [pltpu.make_async_copy(a, b, small.at[i]) for i, (a, b) in enumerate(tables)]
    for copy in tables:
        copy.start()
    copies = []
    for h in range(GROUPS):
        columns = slice(width // GROUPS * h, width // GROUPS * (h + 1))
        pair = [
            pltpu.make_async_copy(source.at[:, columns], held.at[:, columns], done.at[i, h])
            for i, (source, held) in enumerate(((keys_hbm, keys), (values_hbm, values)))
        ]
        copies.append(pair)
        for copy in pair:
            copy.start()
    for copy in tables:
        copy.wait()

    def add(k, total):
        return total + jnp.where(k < here, counts[k], 0)

    offset = CH * lax.fori_loop(0, ranks, add, jnp.int32(0), unroll=8)
    live = CH * counts[here]
    last_start = jnp.int32(-FAR)
    next_start = jnp.int32(FAR)
    for b in range(SESSIONS):
        local = starts[b] - offset
        info[3 + b] = local
        last_start = jnp.maximum(last_start, jnp.where(local <= live - 1, local, -FAR))
        next_start = jnp.minimum(next_start, jnp.where(local >= 0, local, FAR))
    info[0] = last_start
    info[1] = live
    info[2] = next_start
    info[7] = counts[here]

    out[:, part:, :] = jnp.full((ranks, CH, DH), -1.0, jnp.bfloat16)

    def mark(j, carry):
        value = jnp.full((CH, DH), slot[j], jnp.int32)
        out[device[j], part:, :] = value.astype(jnp.float32).astype(jnp.bfloat16)
        return carry

    lax.fori_loop(0, counts[here], mark, 0)

    row = lax.broadcasted_iota(jnp.int32, (rows, DH), 0)
    kept = (row >= last_start) & (row < live)
    each = DH // part
    for h in range(width // DH):
        columns = slice(DH * h, DH * (h + 1))
        if h % (width // DH // GROUPS) == 0:
            for copy in copies[h // (width // DH // GROUPS)]:
                copy.wait()
        phi = jnp.where(kept, feature(keys[:, columns]).astype(jnp.float32), 0.0)
        state = lax.dot_general(
            phi.astype(jnp.bfloat16),
            values[:, columns],
            (((0,), (0,)), ((), ())),
            preferred_element_type=jnp.float32,
        ).astype(jnp.bfloat16)
        for i in range(each):
            out[each * h + i, :part, :] = state[part * i : part * (i + 1), :]


def column_copies(weight, held, done, pieces):
    groups = lax.axis_size("head")
    block = weight.shape[1] // groups
    half = block // 2
    copies = []
    for n, (by, i) in enumerate(pieces):
        column = lax.rem(lax.axis_index("head") + by, groups)
        start = pl.multiple_of(column * block + i * half, half)
        copies.append(
            pltpu.make_async_copy(weight.at[:, pl.ds(start, half)], held.at[n], done.at[n])
        )
    for copy in copies:
        copy.start()
    return copies


def prefix_kernel(
    counts_hbm, starts_hbm, got, weight, out, slots, held, counts, starts, done, held_done
):
    fetches = column_copies(weight, held, held_done, ((2, 0),))
    copies = [
        pltpu.make_async_copy(counts_hbm, counts, done.at[0]),
        pltpu.make_async_copy(starts_hbm, starts, done.at[1]),
    ]
    for copy in copies:
        copy.start()
    ranks, part, _ = out.shape
    lane = lax.broadcasted_iota(jnp.int32, (8, DH), 1)
    gathered = jnp.zeros((8, DH), jnp.float32)
    for k in range(ranks):
        gathered = jnp.where(lane == k, got[k, part:, :].astype(jnp.float32), gathered)
    slots[...] = gathered[:1].astype(jnp.int32)
    for copy in copies:
        copy.wait()
    running = jnp.zeros((part, DH), jnp.float32)
    first = jnp.int32(0)
    for k in range(ranks):
        out[k] = running.astype(jnp.bfloat16)
        after = first + CH * counts[k]
        reset = jnp.int32(0)
        for b in range(SESSIONS):
            reset = reset | ((starts[b] >= first) & (starts[b] < after)).astype(jnp.int32)
        first = after
        if k + 1 < ranks:
            keep = jnp.full((part, DH), 1 - reset, jnp.int32) > 0
            running = jnp.where(keep, running, 0.0) + got[k, :part, :].astype(jnp.float32)
    for fetch in fetches:
        fetch.wait()


def inside_kernel(
    info, queries_hbm, keys_hbm, values_hbm, phi_out, out, queries, keys, values, done
):
    rows, width = queries.shape
    group = width // GROUPS
    copies = []
    for h in range(GROUPS):
        columns = slice(group * h, group * (h + 1))
        pairs = ((queries_hbm, queries), (keys_hbm, keys), (values_hbm, values))
        copies.append(
            [
                pltpu.make_async_copy(source.at[:, columns], held.at[:, columns], done.at[i, h])
                for i, (source, held) in enumerate(pairs)
            ]
        )
        for copy in copies[h]:
            copy.start()
    row = lax.broadcasted_iota(jnp.int32, (rows, 1), 0)
    lower = jnp.full((rows, 1), -FAR, jnp.int32)
    for b in range(SESSIONS):
        lower = jnp.maximum(lower, jnp.where(row >= info[3 + b], info[3 + b], -FAR))
    column = lax.broadcasted_iota(jnp.int32, (rows, rows), 1)
    allowed = (column <= row) & (column >= lower)
    for h in range(width // DH):
        columns = slice(DH * h, DH * (h + 1))
        if DH * h % group == 0:
            for copy in copies[DH * h // group]:
                copy.wait()
        phi_q = feature(queries[:, columns])
        phi_k = feature(keys[:, columns])
        phi_out[:, columns] = phi_q
        scores = lax.dot_general(
            phi_q, phi_k, (((1,), (1,)), ((), ())), preferred_element_type=jnp.float32
        )
        scores = jnp.where(allowed, scores, 0.0).astype(jnp.bfloat16)
        out[:, columns] = jnp.dot(
            scores, values[:, columns], preferred_element_type=jnp.float32
        ).astype(jnp.bfloat16)


def attend_kernel(
    info, device_hbm, phi_q, inside, state, gain, weight, out, kept, scratch, device, done, device_done
):
    table = pltpu.make_async_copy(device_hbm, device, device_done)
    table.start()
    copies = column_copies(weight, kept, done, ((2, 1), (1, 1)))
    rows, width = phi_q.shape
    row = lax.broadcasted_iota(jnp.int32, (rows, 1), 0)
    open_row = row < info[2]
    for h in range(width // DH):
        columns = slice(DH * h, DH * (h + 1))
        carried = jnp.dot(phi_q[:, columns], state[h], preferred_element_type=jnp.float32)
        numer = inside[:, columns].astype(jnp.float32) + jnp.where(open_row, carried, 0.0)
        inverse = lax.rsqrt(jnp.mean(numer * numer, axis=1, keepdims=True) + EPSILON)
        scratch[:, columns] = numer * inverse * gain[:, columns]

    table.wait()

    def place(j, carry):
        start = pl.multiple_of(j * CH, CH)
        out[device[j]] = scratch[pl.ds(start, CH), :].astype(jnp.bfloat16)
        return carry

    lax.fori_loop(0, info[7], place, 0)
    for copy in copies:
        copy.wait()


def product(packed, weight, out):
    out[...] = jnp.dot(packed[...], weight, preferred_element_type=jnp.float32).astype(
        jnp.bfloat16
    )


def across_kernel(
    slots, arrived, for_left, for_right, weight, packed, left, right, later, source, later_done
):
    last = lax.axis_size("head") - 1
    fetches = column_copies(weight, later, later_done, ((last, 0),))
    for s in range(arrived.shape[0]):
        slot = slots[0, s]
        source[jnp.where(slot < 0, BAL, slot)] = jnp.int32(s)
    for i in range(0, BAL, 2):
        packed[CH * i : CH * (i + 2), :] = jnp.concatenate(
            [arrived[source[i]], arrived[source[i + 1]]], axis=0
        )
    product(packed, for_left[0], left)
    product(packed, for_right[0], right)
    for fetch in fetches:
        fetch.wait()


def beside_kernel(packed, for_right, for_behind, weight, ahead_right, behind_left, later, done):
    last = lax.axis_size("head") - 1
    fetches = column_copies(weight, later, done, ((1, 0), (last, 1)))
    product(packed, for_right[1], ahead_right)
    product(packed, for_behind[0], behind_left)
    for fetch in fetches:
        fetch.wait()


def join_kernel(packed, kept, up, down, left, right):
    for n, (arrived, out) in enumerate(((up, left), (down, right))):
        own = jnp.dot(packed[...], kept[n], preferred_element_type=jnp.float32)
        own = own.astype(jnp.bfloat16).astype(jnp.float32)
        out[...] = (own + arrived[...].astype(jnp.float32)).astype(jnp.bfloat16)


def own_kernel(packed, weight, from_ahead, from_behind, left, right, held, done):
    copies = column_copies(weight, held, done, ((0, 0), (0, 1)))
    for n, (arrived, out) in enumerate(((from_ahead, left), (from_behind, right))):
        copies[n].wait()
        own = jnp.dot(packed[...], held[n], preferred_element_type=jnp.float32)
        own = own.astype(jnp.bfloat16).astype(jnp.float32)
        out[...] = own + arrived[...].astype(jnp.float32)


def ctx_exchange(x):
    return lax.all_to_all(x, "ctx", split_axis=0, concat_axis=0, tiled=True)


def head_shift(x, by):
    count = lax.axis_size("head")
    return lax.ppermute(x, "head", [(i, (i + by) % count) for i in range(count)])


def wide(x):
    return x.astype(jnp.float32)


def per_device(
    queries,
    keys,
    values,
    out_weight,
    norm_gain,
    tile_counts,
    route_device,
    route_slot,
    session_starts,
):
    ranks = lax.axis_size("ctx")
    groups = lax.axis_size("head")
    rows, width = queries.shape
    heads = width // DH
    part = heads * DH // ranks
    smem = pl.BlockSpec(memory_space=SMEM)
    vmem = pl.BlockSpec(memory_space=VMEM)
    hbm = pl.BlockSpec(memory_space=HBM)
    in_hbm = lambda x: pltpu.with_memory_space_constraint(x, HBM)
    params = pltpu.CompilerParams(vmem_limit_bytes=16 << 20)

    tables = [in_hbm(x) for x in (tile_counts, session_starts, route_device, route_slot)]
    tile_counts, session_starts, route_device, route_slot = tables
    entry, info = pl.pallas_call(
        entry_kernel,
        in_specs=[hbm] * 6,
        out_specs=[vmem, smem],
        out_shape=[
            jax.ShapeDtypeStruct((ranks, part + CH, DH), jnp.bfloat16),
            jax.ShapeDtypeStruct((8,), jnp.int32),
        ],
        scratch_shapes=[
            pltpu.VMEM((rows, width), keys.dtype),
            pltpu.VMEM((rows, width), values.dtype),
            *[pltpu.SMEM(x.shape, jnp.int32) for x in tables],
            pltpu.SemaphoreType.DMA((2, GROUPS)),
            pltpu.SemaphoreType.DMA((4,)),
        ],
        compiler_params=params,
        name="entry",
    )(*tables, in_hbm(keys), in_hbm(values))

    got = ctx_exchange(entry)

    half = out_weight.shape[1] // groups // 2
    held = lambda n: jax.ShapeDtypeStruct((n, width, half), out_weight.dtype)
    phi_q, inside = pl.pallas_call(
        inside_kernel,
        in_specs=[smem] + [hbm] * 3,
        out_specs=[vmem] * 2,
        out_shape=[jax.ShapeDtypeStruct((rows, width), jnp.bfloat16)] * 2,
        scratch_shapes=[
            *[pltpu.VMEM((rows, width), jnp.bfloat16)] * 3,
            pltpu.SemaphoreType.DMA((3, GROUPS)),
        ],
        compiler_params=params,
        name="inside",
    )(info, in_hbm(queries), in_hbm(keys), in_hbm(values))

    got, phi_q, inside = lax.optimization_barrier((got, phi_q, inside))
    summed, slots, for_left = pl.pallas_call(
        prefix_kernel,
        in_specs=[hbm, hbm, vmem, hbm],
        out_specs=[vmem] * 3,
        out_shape=[
            jax.ShapeDtypeStruct((ranks, part, DH), jnp.bfloat16),
            jax.ShapeDtypeStruct((1, DH), jnp.int32),
            held(1),
        ],
        scratch_shapes=[
            pltpu.SMEM(tile_counts.shape, jnp.int32),
            pltpu.SMEM(session_starts.shape, jnp.int32),
            pltpu.SemaphoreType.DMA((2,)),
            pltpu.SemaphoreType.DMA((1,)),
        ],
        compiler_params=params,
        name="prefix",
    )(tile_counts, session_starts, got, in_hbm(out_weight))

    state = ctx_exchange(summed).reshape(heads, DH, DH)

    payload, for_right = pl.pallas_call(
        attend_kernel,
        in_specs=[smem, hbm] + [vmem] * 4 + [hbm],
        out_specs=[vmem] * 2,
        out_shape=[jax.ShapeDtypeStruct((ranks, CH, width), jnp.bfloat16), held(2)],
        scratch_shapes=[
            pltpu.VMEM((rows, width), jnp.float32),
            pltpu.SMEM(route_device.shape, jnp.int32),
            pltpu.SemaphoreType.DMA((2,)),
            pltpu.SemaphoreType.DMA,
        ],
        compiler_params=params,
        name="attend",
    )(
        info,
        route_device,
        phi_q,
        inside,
        state,
        in_hbm(norm_gain.reshape(1, width)),
        in_hbm(out_weight),
    )

    arrived = ctx_exchange(payload)

    piece = jax.ShapeDtypeStruct((BAL * CH, half), jnp.bfloat16)
    packed, *across, for_behind = pl.pallas_call(
        across_kernel,
        in_specs=[smem] + [vmem] * 3 + [hbm],
        out_specs=[vmem] * 4,
        out_shape=[
            jax.ShapeDtypeStruct((BAL * CH, width), jnp.bfloat16),
            piece,
            piece,
            held(1),
        ],
        scratch_shapes=[pltpu.SMEM((BAL + 1,), jnp.int32), pltpu.SemaphoreType.DMA((1,))],
        compiler_params=params,
        name="across",
    )(slots, arrived, for_left, for_right, in_hbm(out_weight))
    up = head_shift(across[0], 1)
    down = head_shift(across[1], -1)

    ahead_right, behind_left, later = pl.pallas_call(
        beside_kernel,
        in_specs=[vmem] * 3 + [hbm],
        out_specs=[vmem] * 3,
        out_shape=[piece, piece, held(2)],
        scratch_shapes=[pltpu.SemaphoreType.DMA((2,))],
        compiler_params=params,
        name="beside",
    )(packed, for_right, for_behind, in_hbm(out_weight))
    from_behind = head_shift(ahead_right, 1)
    from_ahead = head_shift(behind_left, -1)

    left_sum, right_sum = pl.pallas_call(
        join_kernel,
        in_specs=[vmem] * 4,
        out_specs=[vmem] * 2,
        out_shape=[piece] * 2,
        compiler_params=params,
        name="join",
    )(packed, later, up, down)
    last_left = head_shift(left_sum, 1)
    last_right = head_shift(right_sum, -1)

    left, right = pl.pallas_call(
        own_kernel,
        in_specs=[vmem, hbm, vmem, vmem],
        out_specs=[vmem] * 2,
        out_shape=[jax.ShapeDtypeStruct((BAL * CH, half), jnp.float32)] * 2,
        scratch_shapes=[
            pltpu.VMEM((2, width, half), out_weight.dtype),
            pltpu.SemaphoreType.DMA((2,)),
        ],
        compiler_params=params,
        name="own",
    )(packed, in_hbm(out_weight), from_ahead, from_behind)
    left = left + wide(last_left)
    right = right + wide(last_right)
    return jnp.concatenate([left, right], axis=1).astype(jnp.bfloat16)


def solution(mesh):
    placed = (
        P("ctx", "head"),
        P("ctx", "head"),
        P("ctx", "head"),
        P("head", None),
        P("head"),
        P(),
        P("ctx"),
        P("ctx"),
        P(),
    )
    return jax.shard_map(
        per_device, mesh=mesh, in_specs=placed, out_specs=P("ctx", "head"), check_vma=False
    )
```

```python
import jax
import jax.numpy as jnp
from jax import lax
from jax.experimental import pallas as pl
from jax.experimental.pallas import tpu as pltpu
from jax.sharding import PartitionSpec as P

DH = 128
CH = 8
BAL = 32
SESSIONS = 4
GROUPS = 2
EPSILON = 1e-06
FAR = 1 << 28
SMEM = pltpu.MemorySpace.SMEM
VMEM = pltpu.MemorySpace.VMEM
HBM = pltpu.MemorySpace.HBM


def feature(block):
    value = block.astype(jnp.float32)
    return jnp.where(value > 0, value + 1.0, jnp.exp(jnp.minimum(value, 0.0))).astype(jnp.bfloat16)


def entry_kernel(
    counts_hbm, starts_hbm, device_hbm, slot_hbm, keys_hbm, values_hbm,
    out, info, keys, values, counts, starts, device, slot, done, small,
):
    ranks = counts.shape[0]
    here = lax.axis_index("ctx")
    rows, width = keys.shape
    part = width // ranks
    tables = ((counts_hbm, counts), (starts_hbm, starts), (device_hbm, device), (slot_hbm, slot))
    tables = [pltpu.make_async_copy(a, b, small.at[i]) for i, (a, b) in enumerate(tables)]
    for copy in tables:
        copy.start()
    copies = []
    for h in range(GROUPS):
        columns = slice(width // GROUPS * h, width // GROUPS * (h + 1))
        pair = [
            pltpu.make_async_copy(source.at[:, columns], held.at[:, columns], done.at[i, h])
            for i, (source, held) in enumerate(((keys_hbm, keys), (values_hbm, values)))
        ]
        copies.append(pair)
        for copy in pair:
            copy.start()
    for copy in tables:
        copy.wait()

    def add(k, total):
        return total + jnp.where(k < here, counts[k], 0)

    offset = CH * lax.fori_loop(0, ranks, add, jnp.int32(0), unroll=8)
    live = CH * counts[here]
    last_start = jnp.int32(-FAR)
    next_start = jnp.int32(FAR)
    for b in range(SESSIONS):
        local = starts[b] - offset
        info[3 + b] = local
        last_start = jnp.maximum(last_start, jnp.where(local <= live - 1, local, -FAR))
        next_start = jnp.minimum(next_start, jnp.where(local >= 0, local, FAR))
    info[0] = last_start
    info[1] = live
    info[2] = next_start
    info[7] = counts[here]

    out[:, part // 2 :] = jnp.full((ranks, 1, 2, DH), -1.0, jnp.bfloat16)

    def mark(j, carry):
        value = jnp.full((1, 2, DH), slot[j], jnp.int32)
        out[device[j], part // 2 :] = value.astype(jnp.float32).astype(jnp.bfloat16)
        return carry

    lax.fori_loop(0, counts[here], mark, 0)

    row = lax.broadcasted_iota(jnp.int32, (rows, DH), 0)
    kept = (row >= last_start) & (row < live)
    each = DH // part
    for h in range(width // DH):
        columns = slice(DH * h, DH * (h + 1))
        if h % (width // DH // GROUPS) == 0:
            for copy in copies[h // (width // DH // GROUPS)]:
                copy.wait()
        phi = jnp.where(kept, feature(keys[:, columns]).astype(jnp.float32), 0.0)
        state = lax.dot_general(
            phi.astype(jnp.bfloat16),
            values[:, columns],
            (((0,), (0,)), ((), ())),
            preferred_element_type=jnp.float32,
        ).astype(jnp.bfloat16)
        for i in range(each):
            out[each * h + i, : part // 2] = state[part * i : part * (i + 1), :].reshape(part // 2, 2, DH)


def column_copies(weight, held, done, pieces):
    groups = lax.axis_size("head")
    block = weight.shape[1] // groups
    half = block // 2
    copies = []
    for n, (by, i) in enumerate(pieces):
        column = lax.rem(lax.axis_index("head") + by, groups)
        start = pl.multiple_of(column * block + i * half, half)
        copies.append(
            pltpu.make_async_copy(weight.at[:, pl.ds(start, half)], held.at[n], done.at[n])
        )
    for copy in copies:
        copy.start()
    return copies


def prefix_kernel(
    counts_hbm, starts_hbm, got, weight, out, slots, held, counts, starts, done, held_done
):
    fetches = column_copies(weight, held, held_done, ((2, 0), (2, 1)))
    copies = [
        pltpu.make_async_copy(counts_hbm, counts, done.at[0]),
        pltpu.make_async_copy(starts_hbm, starts, done.at[1]),
    ]
    for copy in copies:
        copy.start()
    ranks, part, _ = out.shape
    lane = lax.broadcasted_iota(jnp.int32, (2, DH), 1)
    gathered = jnp.zeros((2, DH), jnp.float32)
    for k in range(ranks):
        gathered = jnp.where(lane == k, got[k, part // 2].astype(jnp.float32), gathered)
    slots[...] = gathered[:1].astype(jnp.int32)
    for copy in copies:
        copy.wait()
    running = jnp.zeros((part, DH), jnp.float32)
    first = jnp.int32(0)
    for k in range(ranks):
        out[k] = running.astype(jnp.bfloat16)
        after = first + CH * counts[k]
        reset = jnp.int32(0)
        for b in range(SESSIONS):
            reset = reset | ((starts[b] >= first) & (starts[b] < after)).astype(jnp.int32)
        first = after
        if k + 1 < ranks:
            keep = jnp.full((part, DH), 1 - reset, jnp.int32) > 0
            running = jnp.where(keep, running, 0.0) + got[k, : part // 2].reshape(part, DH).astype(jnp.float32)
    for fetch in fetches:
        fetch.wait()


def inside_kernel(
    info, queries_hbm, keys_hbm, values_hbm, phi_out, out, queries, keys, values, done
):
    rows, width = queries.shape
    group = width // GROUPS
    copies = []
    for h in range(GROUPS):
        columns = slice(group * h, group * (h + 1))
        pairs = ((queries_hbm, queries), (keys_hbm, keys), (values_hbm, values))
        copies.append(
            [
                pltpu.make_async_copy(source.at[:, columns], held.at[:, columns], done.at[i, h])
                for i, (source, held) in enumerate(pairs)
            ]
        )
        for copy in copies[h]:
            copy.start()
    row = lax.broadcasted_iota(jnp.int32, (rows, 1), 0)
    lower = jnp.full((rows, 1), -FAR, jnp.int32)
    for b in range(SESSIONS):
        lower = jnp.maximum(lower, jnp.where(row >= info[3 + b], info[3 + b], -FAR))
    column = lax.broadcasted_iota(jnp.int32, (rows, rows), 1)
    allowed = (column <= row) & (column >= lower)
    for h in range(width // DH):
        columns = slice(DH * h, DH * (h + 1))
        if DH * h % group == 0:
            for copy in copies[DH * h // group]:
                copy.wait()
        phi_q = feature(queries[:, columns])
        phi_k = feature(keys[:, columns])
        phi_out[:, columns] = phi_q
        scores = lax.dot_general(
            phi_q, phi_k, (((1,), (1,)), ((), ())), preferred_element_type=jnp.float32
        )
        scores = jnp.where(allowed, scores, 0.0).astype(jnp.bfloat16)
        out[:, columns] = jnp.dot(
            scores, values[:, columns], preferred_element_type=jnp.float32
        ).astype(jnp.bfloat16)


def attend_kernel(
    info, device_hbm, phi_q, inside, state, gain, out, scratch, device, device_done
):
    table = pltpu.make_async_copy(device_hbm, device, device_done)
    table.start()
    rows, width = phi_q.shape
    row = lax.broadcasted_iota(jnp.int32, (rows, 1), 0)
    open_row = row < info[2]
    for h in range(width // DH):
        columns = slice(DH * h, DH * (h + 1))
        carried = jnp.dot(phi_q[:, columns], state[h], preferred_element_type=jnp.float32)
        numer = inside[:, columns].astype(jnp.float32) + jnp.where(open_row, carried, 0.0)
        inverse = lax.rsqrt(jnp.mean(numer * numer, axis=1, keepdims=True) + EPSILON)
        scratch[:, columns] = numer * inverse * gain[:, columns]

    table.wait()

    def place(j, carry):
        start = pl.multiple_of(j * CH, CH)
        out[device[j]] = scratch[pl.ds(start, CH), :].astype(jnp.bfloat16)
        return carry

    lax.fori_loop(0, info[7], place, 0)


def product(packed, weight, out):
    out[...] = jnp.dot(packed[...], weight, preferred_element_type=jnp.float32).astype(
        jnp.bfloat16
    )


def across_kernel(slots, arrived, for_across, packed, left, right, source):
    for s in range(arrived.shape[0]):
        slot = slots[0, s]
        source[jnp.where(slot < 0, BAL, slot)] = jnp.int32(s)
    for i in range(0, BAL, 2):
        packed[CH * i : CH * (i + 2), :] = jnp.concatenate(
            [arrived[source[i]], arrived[source[i + 1]]], axis=0
        )
    product(packed, for_across[0], left)
    product(packed, for_across[1], right)


def beside_kernel(packed, weight, ahead_right, behind_left, later, held, later_done, done):
    last = lax.axis_size("head") - 1
    copies = column_copies(weight, held, done, ((1, 1), (last, 0)))
    fetches = column_copies(weight, later, later_done, ((1, 0), (last, 1)))
    for n, out in enumerate((ahead_right, behind_left)):
        copies[n].wait()
        product(packed, held[n], out)
    for fetch in fetches:
        fetch.wait()


def join_kernel(packed, kept, up, down, left, right):
    for n, (arrived, out) in enumerate(((up, left), (down, right))):
        own = jnp.dot(packed[...], kept[n], preferred_element_type=jnp.float32)
        own = own.astype(jnp.bfloat16).astype(jnp.float32)
        out[...] = (own + arrived[...].astype(jnp.float32)).astype(jnp.bfloat16)


def own_kernel(packed, weight, from_ahead, from_behind, left, right, held, done):
    copies = column_copies(weight, held, done, ((0, 0), (0, 1)))
    for n, (arrived, out) in enumerate(((from_ahead, left), (from_behind, right))):
        copies[n].wait()
        own = jnp.dot(packed[...], held[n], preferred_element_type=jnp.float32)
        own = own.astype(jnp.bfloat16).astype(jnp.float32)
        out[...] = own + arrived[...].astype(jnp.float32)


def ctx_exchange(x):
    return lax.all_to_all(x, "ctx", split_axis=0, concat_axis=0, tiled=True)


def head_shift(x, by):
    count = lax.axis_size("head")
    return lax.ppermute(x, "head", [(i, (i + by) % count) for i in range(count)])


def wide(x):
    return x.astype(jnp.float32)


def per_device(
    queries,
    keys,
    values,
    out_weight,
    norm_gain,
    tile_counts,
    route_device,
    route_slot,
    session_starts,
):
    ranks = lax.axis_size("ctx")
    groups = lax.axis_size("head")
    rows, width = queries.shape
    heads = width // DH
    part = heads * DH // ranks
    smem = pl.BlockSpec(memory_space=SMEM)
    vmem = pl.BlockSpec(memory_space=VMEM)
    hbm = pl.BlockSpec(memory_space=HBM)
    in_hbm = lambda x: pltpu.with_memory_space_constraint(x, HBM)
    params = pltpu.CompilerParams(vmem_limit_bytes=16 << 20)

    tables = [in_hbm(x) for x in (tile_counts, session_starts, route_device, route_slot)]
    tile_counts, session_starts, route_device, route_slot = tables
    entry, info = pl.pallas_call(
        entry_kernel,
        in_specs=[hbm] * 6,
        out_specs=[vmem, smem],
        out_shape=[
            jax.ShapeDtypeStruct((ranks, part // 2 + 1, 2, DH), jnp.bfloat16),
            jax.ShapeDtypeStruct((8,), jnp.int32),
        ],
        scratch_shapes=[
            pltpu.VMEM((rows, width), keys.dtype),
            pltpu.VMEM((rows, width), values.dtype),
            *[pltpu.SMEM(x.shape, jnp.int32) for x in tables],
            pltpu.SemaphoreType.DMA((2, GROUPS)),
            pltpu.SemaphoreType.DMA((4,)),
        ],
        compiler_params=params,
        name="entry",
    )(*tables, in_hbm(keys), in_hbm(values))

    got = ctx_exchange(entry)

    half = out_weight.shape[1] // groups // 2
    held = lambda n: jax.ShapeDtypeStruct((n, width, half), out_weight.dtype)
    phi_q, inside = pl.pallas_call(
        inside_kernel,
        in_specs=[smem] + [hbm] * 3,
        out_specs=[vmem] * 2,
        out_shape=[jax.ShapeDtypeStruct((rows, width), jnp.bfloat16)] * 2,
        scratch_shapes=[
            *[pltpu.VMEM((rows, width), jnp.bfloat16)] * 3,
            pltpu.SemaphoreType.DMA((3, GROUPS)),
        ],
        compiler_params=params,
        name="inside",
    )(info, in_hbm(queries), in_hbm(keys), in_hbm(values))

    got, phi_q, inside = lax.optimization_barrier((got, phi_q, inside))
    summed, slots, for_across = pl.pallas_call(
        prefix_kernel,
        in_specs=[hbm, hbm, vmem, hbm],
        out_specs=[vmem] * 3,
        out_shape=[
            jax.ShapeDtypeStruct((ranks, part, DH), jnp.bfloat16),
            jax.ShapeDtypeStruct((1, DH), jnp.int32),
            held(2),
        ],
        scratch_shapes=[
            pltpu.SMEM(tile_counts.shape, jnp.int32),
            pltpu.SMEM(session_starts.shape, jnp.int32),
            pltpu.SemaphoreType.DMA((2,)),
            pltpu.SemaphoreType.DMA((2,)),
        ],
        compiler_params=params,
        name="prefix",
    )(tile_counts, session_starts, got, in_hbm(out_weight))

    state = ctx_exchange(summed).reshape(heads, DH, DH)

    payload = pl.pallas_call(
        attend_kernel,
        in_specs=[smem, hbm] + [vmem] * 4,
        out_specs=vmem,
        out_shape=jax.ShapeDtypeStruct((ranks, CH, width), jnp.bfloat16),
        scratch_shapes=[
            pltpu.VMEM((rows, width), jnp.float32),
            pltpu.SMEM(route_device.shape, jnp.int32),
            pltpu.SemaphoreType.DMA,
        ],
        compiler_params=params,
        name="attend",
    )(info, route_device, phi_q, inside, state, in_hbm(norm_gain.reshape(1, width)))

    arrived = ctx_exchange(payload)

    piece = jax.ShapeDtypeStruct((BAL * CH, half), jnp.bfloat16)
    packed, *across = pl.pallas_call(
        across_kernel,
        in_specs=[smem] + [vmem] * 2,
        out_specs=[vmem] * 3,
        out_shape=[jax.ShapeDtypeStruct((BAL * CH, width), jnp.bfloat16), piece, piece],
        scratch_shapes=[pltpu.SMEM((BAL + 1,), jnp.int32)],
        compiler_params=params,
        name="across",
    )(slots, arrived, for_across)
    up = head_shift(across[0], 1)
    down = head_shift(across[1], -1)

    ahead_right, behind_left, later = pl.pallas_call(
        beside_kernel,
        in_specs=[vmem, hbm],
        out_specs=[vmem] * 3,
        out_shape=[piece, piece, held(2)],
        scratch_shapes=[
            pltpu.VMEM((2, width, half), out_weight.dtype),
            pltpu.SemaphoreType.DMA((2,)),
            pltpu.SemaphoreType.DMA((2,)),
        ],
        compiler_params=params,
        name="beside",
    )(packed, in_hbm(out_weight))
    from_behind = head_shift(ahead_right, 1)
    from_ahead = head_shift(behind_left, -1)

    left_sum, right_sum = pl.pallas_call(
        join_kernel,
        in_specs=[vmem] * 4,
        out_specs=[vmem] * 2,
        out_shape=[piece] * 2,
        compiler_params=params,
        name="join",
    )(packed, later, up, down)
    last_left = head_shift(left_sum, 1)
    last_right = head_shift(right_sum, -1)

    left, right = pl.pallas_call(
        own_kernel,
        in_specs=[vmem, hbm, vmem, vmem],
        out_specs=[vmem] * 2,
        out_shape=[jax.ShapeDtypeStruct((BAL * CH, half), jnp.float32)] * 2,
        scratch_shapes=[
            pltpu.VMEM((2, width, half), out_weight.dtype),
            pltpu.SemaphoreType.DMA((2,)),
        ],
        compiler_params=params,
        name="own",
    )(packed, in_hbm(out_weight), from_ahead, from_behind)
    left = left + wide(last_left)
    right = right + wide(last_right)
    return jnp.concatenate([left, right], axis=1).astype(jnp.bfloat16)


def solution(mesh):
    placed = (
        P("ctx", "head"),
        P("ctx", "head"),
        P("ctx", "head"),
        P("head", None),
        P("head"),
        P(),
        P("ctx"),
        P("ctx"),
        P(),
    )
    return jax.shard_map(
        per_device, mesh=mesh, in_specs=placed, out_specs=P("ctx", "head"), check_vma=False
    )
```

```python
import jax
import jax.numpy as jnp
from jax import lax
from jax.experimental import pallas as pl
from jax.experimental.pallas import tpu as pltpu
from jax.sharding import PartitionSpec as P

DH = 128
CH = 8
BAL = 32
SESSIONS = 4
GROUPS = 2
EPSILON = 1e-06
FAR = 1 << 28
SMEM = pltpu.MemorySpace.SMEM
VMEM = pltpu.MemorySpace.VMEM
HBM = pltpu.MemorySpace.HBM


def feature(block):
    value = block.astype(jnp.float32)
    return jnp.where(value > 0, value + 1.0, jnp.exp(jnp.minimum(value, 0.0))).astype(jnp.bfloat16)


def entry_kernel(
    counts_hbm, starts_hbm, device_hbm, slot_hbm, keys_hbm, values_hbm,
    out, info, keys, values, counts, starts, device, slot, done, small,
):
    ranks = counts.shape[0]
    here = lax.axis_index("ctx")
    rows, width = keys.shape
    part = width // ranks
    tables = ((counts_hbm, counts), (starts_hbm, starts), (device_hbm, device), (slot_hbm, slot))
    tables = [pltpu.make_async_copy(a, b, small.at[i]) for i, (a, b) in enumerate(tables)]
    for copy in tables:
        copy.start()
    copies = []
    for h in range(GROUPS):
        columns = slice(width // GROUPS * h, width // GROUPS * (h + 1))
        pair = [
            pltpu.make_async_copy(source.at[:, columns], held.at[:, columns], done.at[i, h])
            for i, (source, held) in enumerate(((keys_hbm, keys), (values_hbm, values)))
        ]
        copies.append(pair)
        for copy in pair:
            copy.start()
    for copy in tables:
        copy.wait()

    def add(k, total):
        return total + jnp.where(k < here, counts[k], 0)

    offset = CH * lax.fori_loop(0, ranks, add, jnp.int32(0), unroll=8)
    live = CH * counts[here]
    last_start = jnp.int32(-FAR)
    next_start = jnp.int32(FAR)
    for b in range(SESSIONS):
        local = starts[b] - offset
        info[3 + b] = local
        last_start = jnp.maximum(last_start, jnp.where(local <= live - 1, local, -FAR))
        next_start = jnp.minimum(next_start, jnp.where(local >= 0, local, FAR))
    info[0] = last_start
    info[1] = live
    info[2] = next_start
    info[7] = counts[here]

    out[:, part // 2 :] = jnp.full((ranks, 1, 2, DH), -1.0, jnp.bfloat16)

    def mark(j, carry):
        value = jnp.full((1, 2, DH), slot[j], jnp.int32)
        out[device[j], part // 2 :] = value.astype(jnp.float32).astype(jnp.bfloat16)
        return carry

    lax.fori_loop(0, counts[here], mark, 0)

    row = lax.broadcasted_iota(jnp.int32, (rows, DH), 0)
    kept = (row >= last_start) & (row < live)
    each = DH // part
    for h in range(width // DH):
        columns = slice(DH * h, DH * (h + 1))
        if h % (width // DH // GROUPS) == 0:
            for copy in copies[h // (width // DH // GROUPS)]:
                copy.wait()
        phi = jnp.where(kept, feature(keys[:, columns]).astype(jnp.float32), 0.0)
        state = lax.dot_general(
            phi.astype(jnp.bfloat16),
            values[:, columns],
            (((0,), (0,)), ((), ())),
            preferred_element_type=jnp.float32,
        ).astype(jnp.bfloat16)
        for i in range(each):
            out[each * h + i, : part // 2] = state[part * i : part * (i + 1), :].reshape(part // 2, 2, DH)


def column_copies(weight, held, done, pieces):
    groups = lax.axis_size("head")
    block = weight.shape[1] // groups
    half = block // 2
    copies = []
    for n, (by, i) in enumerate(pieces):
        column = lax.rem(lax.axis_index("head") + by, groups)
        start = pl.multiple_of(column * block + i * half, half)
        copies.append(
            pltpu.make_async_copy(weight.at[:, pl.ds(start, half)], held.at[n], done.at[n])
        )
    for copy in copies:
        copy.start()
    return copies


def prefix_kernel(resets, got, weight, out, slots, held, held_done):
    fetches = column_copies(weight, held, held_done, ((2, 0), (2, 1)))
    ranks, part, _ = out.shape
    lane = lax.broadcasted_iota(jnp.int32, (2, DH), 1)
    gathered = jnp.zeros((2, DH), jnp.float32)
    for k in range(ranks):
        gathered = jnp.where(lane == k, got[k, part // 2].astype(jnp.float32), gathered)
    slots[...] = gathered[:1].astype(jnp.int32)
    running = jnp.zeros((part, DH), jnp.float32)
    for k in range(ranks):
        out[k] = running.astype(jnp.bfloat16)
        if k + 1 < ranks:
            keep = jnp.full((part, DH), 1 - resets[k], jnp.int32) > 0
            entry = got[k, : part // 2].reshape(part, DH).astype(jnp.float32)
            running = jnp.where(keep, running, 0.0) + entry
    for fetch in fetches:
        fetch.wait()


def inside_kernel(
    info, counts, starts, device, gain_hbm, queries_hbm, keys_hbm, values_hbm,
    phi_out, out, near, route, gain,
    queries, keys, values, done, gain_done,
):
    rows, width = queries.shape
    group = width // GROUPS
    copies = []
    for h in range(GROUPS):
        columns = slice(group * h, group * (h + 1))
        pairs = ((queries_hbm, queries), (keys_hbm, keys), (values_hbm, values))
        copies.append(
            [
                pltpu.make_async_copy(source.at[:, columns], held.at[:, columns], done.at[i, h])
                for i, (source, held) in enumerate(pairs)
            ]
        )
        for copy in copies[h]:
            copy.start()
    gain_copy = pltpu.make_async_copy(gain_hbm, gain, gain_done)
    gain_copy.start()

    def flag(k, first):
        after = first + CH * counts[k]
        reset = jnp.int32(0)
        for b in range(SESSIONS):
            reset = reset | ((starts[b] >= first) & (starts[b] < after)).astype(jnp.int32)
        near[k] = reset
        return after

    lax.fori_loop(0, counts.shape[0], flag, jnp.int32(0))

    def note(j, carry):
        route[j] = device[j]
        return carry

    lax.fori_loop(0, device.shape[0], note, 0)
    row = lax.broadcasted_iota(jnp.int32, (rows, 1), 0)
    lower = jnp.full((rows, 1), -FAR, jnp.int32)
    for b in range(SESSIONS):
        lower = jnp.maximum(lower, jnp.where(row >= info[3 + b], info[3 + b], -FAR))
    column = lax.broadcasted_iota(jnp.int32, (rows, rows), 1)
    allowed = (column <= row) & (column >= lower)
    for h in range(width // DH):
        columns = slice(DH * h, DH * (h + 1))
        if DH * h % group == 0:
            for copy in copies[DH * h // group]:
                copy.wait()
        phi_q = feature(queries[:, columns])
        phi_k = feature(keys[:, columns])
        phi_out[:, columns] = phi_q
        scores = lax.dot_general(
            phi_q, phi_k, (((1,), (1,)), ((), ())), preferred_element_type=jnp.float32
        )
        scores = jnp.where(allowed, scores, 0.0).astype(jnp.bfloat16)
        out[:, columns] = jnp.dot(
            scores, values[:, columns], preferred_element_type=jnp.float32
        ).astype(jnp.bfloat16)
    gain_copy.wait()


def attend_kernel(
    info, device, phi_q, inside, state, gain, out, scratch
):
    rows, width = phi_q.shape
    row = lax.broadcasted_iota(jnp.int32, (rows, 1), 0)
    open_row = row < info[2]
    for h in range(width // DH):
        columns = slice(DH * h, DH * (h + 1))
        carried = jnp.dot(phi_q[:, columns], state[h], preferred_element_type=jnp.float32)
        numer = inside[:, columns].astype(jnp.float32) + jnp.where(open_row, carried, 0.0)
        inverse = lax.rsqrt(jnp.mean(numer * numer, axis=1, keepdims=True) + EPSILON)
        scratch[:, columns] = numer * inverse * gain[:, columns]

    def place(j, carry):
        start = pl.multiple_of(j * CH, CH)
        out[device[j]] = scratch[pl.ds(start, CH), :].astype(jnp.bfloat16)
        return carry

    lax.fori_loop(0, info[7], place, 0)


def product(packed, weight, out):
    out[...] = jnp.dot(packed[...], weight, preferred_element_type=jnp.float32).astype(
        jnp.bfloat16
    )


def across_kernel(slots, arrived, for_across, packed, left, right, source):
    for s in range(arrived.shape[0]):
        slot = slots[0, s]
        source[jnp.where(slot < 0, BAL, slot)] = jnp.int32(s)
    for i in range(0, BAL, 2):
        packed[CH * i : CH * (i + 2), :] = jnp.concatenate(
            [arrived[source[i]], arrived[source[i + 1]]], axis=0
        )
    product(packed, for_across[0], left)
    product(packed, for_across[1], right)


def beside_kernel(packed, weight, ahead_right, behind_left, later, held, later_done, done):
    last = lax.axis_size("head") - 1
    copies = column_copies(weight, held, done, ((1, 1), (last, 0)))
    fetches = column_copies(weight, later, later_done, ((1, 0), (last, 1)))
    for n, out in enumerate((ahead_right, behind_left)):
        copies[n].wait()
        product(packed, held[n], out)
    for fetch in fetches:
        fetch.wait()


def join_kernel(packed, kept, up, down, left, right):
    for n, (arrived, out) in enumerate(((up, left), (down, right))):
        own = jnp.dot(packed[...], kept[n], preferred_element_type=jnp.float32)
        own = own.astype(jnp.bfloat16).astype(jnp.float32)
        out[...] = (own + arrived[...].astype(jnp.float32)).astype(jnp.bfloat16)


def own_kernel(packed, weight, from_ahead, from_behind, left, right, held, done):
    copies = column_copies(weight, held, done, ((0, 0), (0, 1)))
    for n, (arrived, out) in enumerate(((from_ahead, left), (from_behind, right))):
        copies[n].wait()
        own = jnp.dot(packed[...], held[n], preferred_element_type=jnp.float32)
        own = own.astype(jnp.bfloat16).astype(jnp.float32)
        out[...] = own + arrived[...].astype(jnp.float32)


def ctx_exchange(x):
    return lax.all_to_all(x, "ctx", split_axis=0, concat_axis=0, tiled=True)


def head_shift(x, by):
    count = lax.axis_size("head")
    return lax.ppermute(x, "head", [(i, (i + by) % count) for i in range(count)])


def wide(x):
    return x.astype(jnp.float32)


def per_device(
    queries,
    keys,
    values,
    out_weight,
    norm_gain,
    tile_counts,
    route_device,
    route_slot,
    session_starts,
):
    ranks = lax.axis_size("ctx")
    groups = lax.axis_size("head")
    rows, width = queries.shape
    heads = width // DH
    part = heads * DH // ranks
    smem = pl.BlockSpec(memory_space=SMEM)
    vmem = pl.BlockSpec(memory_space=VMEM)
    hbm = pl.BlockSpec(memory_space=HBM)
    in_hbm = lambda x: pltpu.with_memory_space_constraint(x, HBM)
    params = pltpu.CompilerParams(vmem_limit_bytes=16 << 20)

    tables = [in_hbm(x) for x in (tile_counts, session_starts, route_device, route_slot)]
    tile_counts, session_starts, route_device, route_slot = tables
    entry, info = pl.pallas_call(
        entry_kernel,
        in_specs=[hbm] * 6,
        out_specs=[vmem, smem],
        out_shape=[
            jax.ShapeDtypeStruct((ranks, part // 2 + 1, 2, DH), jnp.bfloat16),
            jax.ShapeDtypeStruct((8,), jnp.int32),
        ],
        scratch_shapes=[
            pltpu.VMEM((rows, width), keys.dtype),
            pltpu.VMEM((rows, width), values.dtype),
            *[pltpu.SMEM(x.shape, jnp.int32) for x in tables],
            pltpu.SemaphoreType.DMA((2, GROUPS)),
            pltpu.SemaphoreType.DMA((4,)),
        ],
        compiler_params=params,
        name="entry",
    )(*tables, in_hbm(keys), in_hbm(values))

    got = ctx_exchange(entry)

    half = out_weight.shape[1] // groups // 2
    held = lambda n: jax.ShapeDtypeStruct((n, width, half), out_weight.dtype)
    phi_q, inside, resets, route, gain = pl.pallas_call(
        inside_kernel,
        in_specs=[smem] * 4 + [hbm] * 4,
        out_specs=[vmem] * 2 + [smem] * 2 + [vmem] * 1,
        out_shape=[
            jax.ShapeDtypeStruct((rows, width), jnp.bfloat16),
            jax.ShapeDtypeStruct((rows, width), jnp.bfloat16),
            jax.ShapeDtypeStruct(tile_counts.shape, jnp.int32),
            jax.ShapeDtypeStruct(route_device.shape, jnp.int32),
            jax.ShapeDtypeStruct((1, width), jnp.float32),
        ],
        scratch_shapes=[
            *[pltpu.VMEM((rows, width), jnp.bfloat16)] * 3,
            pltpu.SemaphoreType.DMA((3, GROUPS)),
            pltpu.SemaphoreType.DMA,
        ],
        compiler_params=params,
        name="inside",
    )(
        info,
        tile_counts,
        session_starts,
        route_device,
        in_hbm(norm_gain.reshape(1, width)),
        in_hbm(queries),
        in_hbm(keys),
        in_hbm(values),
    )

    got, phi_q, inside, resets = lax.optimization_barrier((got, phi_q, inside, resets))
    summed, slots, for_across = pl.pallas_call(
        prefix_kernel,
        in_specs=[smem, vmem, hbm],
        out_specs=[vmem] * 3,
        out_shape=[
            jax.ShapeDtypeStruct((ranks, part, DH), jnp.bfloat16),
            jax.ShapeDtypeStruct((1, DH), jnp.int32),
            held(2),
        ],
        scratch_shapes=[pltpu.SemaphoreType.DMA((2,))],
        compiler_params=params,
        name="prefix",
    )(resets, got, in_hbm(out_weight))

    state = ctx_exchange(summed).reshape(heads, DH, DH)

    payload = pl.pallas_call(
        attend_kernel,
        in_specs=[smem] * 2 + [vmem] * 4,
        out_specs=vmem,
        out_shape=jax.ShapeDtypeStruct((ranks, CH, width), jnp.bfloat16),
        scratch_shapes=[pltpu.VMEM((rows, width), jnp.float32)],
        compiler_params=params,
        name="attend",
    )(info, route, phi_q, inside, state, gain)

    arrived = ctx_exchange(payload)

    piece = jax.ShapeDtypeStruct((BAL * CH, half), jnp.bfloat16)
    packed, *across = pl.pallas_call(
        across_kernel,
        in_specs=[smem] + [vmem] * 2,
        out_specs=[vmem] * 3,
        out_shape=[jax.ShapeDtypeStruct((BAL * CH, width), jnp.bfloat16), piece, piece],
        scratch_shapes=[pltpu.SMEM((BAL + 1,), jnp.int32)],
        compiler_params=params,
        name="across",
    )(slots, arrived, for_across)
    up = head_shift(across[0], 1)
    down = head_shift(across[1], -1)

    ahead_right, behind_left, later = pl.pallas_call(
        beside_kernel,
        in_specs=[vmem, hbm],
        out_specs=[vmem] * 3,
        out_shape=[piece, piece, held(2)],
        scratch_shapes=[
            pltpu.VMEM((2, width, half), out_weight.dtype),
            pltpu.SemaphoreType.DMA((2,)),
            pltpu.SemaphoreType.DMA((2,)),
        ],
        compiler_params=params,
        name="beside",
    )(packed, in_hbm(out_weight))
    from_behind = head_shift(ahead_right, 1)
    from_ahead = head_shift(behind_left, -1)

    left_sum, right_sum = pl.pallas_call(
        join_kernel,
        in_specs=[vmem] * 4,
        out_specs=[vmem] * 2,
        out_shape=[piece] * 2,
        compiler_params=params,
        name="join",
    )(packed, later, up, down)
    last_left = head_shift(left_sum, 1)
    last_right = head_shift(right_sum, -1)

    left, right = pl.pallas_call(
        own_kernel,
        in_specs=[vmem, hbm, vmem, vmem],
        out_specs=[vmem] * 2,
        out_shape=[jax.ShapeDtypeStruct((BAL * CH, half), jnp.float32)] * 2,
        scratch_shapes=[
            pltpu.VMEM((2, width, half), out_weight.dtype),
            pltpu.SemaphoreType.DMA((2,)),
        ],
        compiler_params=params,
        name="own",
    )(packed, in_hbm(out_weight), from_ahead, from_behind)
    left = left + wide(last_left)
    right = right + wide(last_right)
    return jnp.concatenate([left, right], axis=1).astype(jnp.bfloat16)


def solution(mesh):
    placed = (
        P("ctx", "head"),
        P("ctx", "head"),
        P("ctx", "head"),
        P("head", None),
        P("head"),
        P(),
        P("ctx"),
        P("ctx"),
        P(),
    )
    return jax.shard_map(
        per_device, mesh=mesh, in_specs=placed, out_specs=P("ctx", "head"), check_vma=False
    )
```

```python
import jax
import jax.numpy as jnp
from jax import lax
from jax.experimental import pallas as pl
from jax.experimental.pallas import tpu as pltpu
from jax.sharding import PartitionSpec as P

DH = 128
CH = 8
BAL = 32
SESSIONS = 4
GROUPS = 2
EPSILON = 1e-06
FAR = 1 << 28
SMEM = pltpu.MemorySpace.SMEM
VMEM = pltpu.MemorySpace.VMEM
HBM = pltpu.MemorySpace.HBM


def feature(block):
    value = block.astype(jnp.float32)
    return jnp.where(value > 0, value + 1.0, jnp.exp(jnp.minimum(value, 0.0))).astype(jnp.bfloat16)


def entry_kernel(
    counts_hbm, starts_hbm, device_hbm, slot_hbm, keys_hbm, values_hbm,
    out, info, keys, values, counts, starts, device, slot, done, small,
):
    ranks = counts.shape[0]
    here = lax.axis_index("ctx")
    rows, width = keys.shape
    part = width // ranks
    tables = ((counts_hbm, counts), (starts_hbm, starts), (device_hbm, device), (slot_hbm, slot))
    tables = [pltpu.make_async_copy(a, b, small.at[i]) for i, (a, b) in enumerate(tables)]
    for copy in tables:
        copy.start()
    copies = []
    for h in range(GROUPS):
        columns = slice(width // GROUPS * h, width // GROUPS * (h + 1))
        pair = [
            pltpu.make_async_copy(source.at[:, columns], held.at[:, columns], done.at[i, h])
            for i, (source, held) in enumerate(((keys_hbm, keys), (values_hbm, values)))
        ]
        copies.append(pair)
        for copy in pair:
            copy.start()
    for copy in tables:
        copy.wait()

    def add(k, total):
        return total + jnp.where(k < here, counts[k], 0)

    offset = CH * lax.fori_loop(0, ranks, add, jnp.int32(0), unroll=8)
    live = CH * counts[here]
    last_start = jnp.int32(-FAR)
    next_start = jnp.int32(FAR)
    for b in range(SESSIONS):
        local = starts[b] - offset
        info[3 + b] = local
        last_start = jnp.maximum(last_start, jnp.where(local <= live - 1, local, -FAR))
        next_start = jnp.minimum(next_start, jnp.where(local >= 0, local, FAR))
    info[0] = last_start
    info[1] = live
    info[2] = next_start
    info[7] = counts[here]

    out[:, part // 2 :] = jnp.full((ranks, 1, 2, DH), -1.0, jnp.bfloat16)

    def mark(j, carry):
        value = jnp.full((1, 2, DH), slot[j], jnp.int32)
        out[device[j], part // 2 :] = value.astype(jnp.float32).astype(jnp.bfloat16)
        return carry

    lax.fori_loop(0, counts[here], mark, 0)

    row = lax.broadcasted_iota(jnp.int32, (rows, DH), 0)
    kept = (row >= last_start) & (row < live)
    each = DH // part
    for h in range(width // DH):
        columns = slice(DH * h, DH * (h + 1))
        if h % (width // DH // GROUPS) == 0:
            for copy in copies[h // (width // DH // GROUPS)]:
                copy.wait()
        phi = jnp.where(kept, feature(keys[:, columns]).astype(jnp.float32), 0.0)
        state = lax.dot_general(
            phi.astype(jnp.bfloat16),
            values[:, columns],
            (((0,), (0,)), ((), ())),
            preferred_element_type=jnp.float32,
        ).astype(jnp.bfloat16)
        for i in range(each):
            out[each * h + i, : part // 2] = state[part * i : part * (i + 1), :].reshape(part // 2, 2, DH)


def column_copies(weight, held, done, pieces):
    groups = lax.axis_size("head")
    block = weight.shape[1] // groups
    half = block // 2
    copies = []
    for n, (by, i) in enumerate(pieces):
        column = lax.rem(lax.axis_index("head") + by, groups)
        start = pl.multiple_of(column * block + i * half, half)
        copies.append(
            pltpu.make_async_copy(weight.at[:, pl.ds(start, half)], held.at[n], done.at[n])
        )
    for copy in copies:
        copy.start()
    return copies


def prefix_kernel(resets, got, out, slots):
    ranks, part, _ = out.shape
    lane = lax.broadcasted_iota(jnp.int32, (2, DH), 1)
    gathered = jnp.zeros((2, DH), jnp.float32)
    for k in range(ranks):
        gathered = jnp.where(lane == k, got[k, part // 2].astype(jnp.float32), gathered)
    slots[...] = gathered[:1].astype(jnp.int32)
    running = jnp.zeros((part, DH), jnp.float32)
    for k in range(ranks):
        out[k] = running.astype(jnp.bfloat16)
        if k + 1 < ranks:
            keep = jnp.full((part, DH), 1 - resets[k], jnp.int32) > 0
            entry = got[k, : part // 2].reshape(part, DH).astype(jnp.float32)
            running = jnp.where(keep, running, 0.0) + entry


def inside_kernel(
    info, counts, starts, device, gain_hbm, queries_hbm, keys_hbm, values_hbm, weight,
    phi_out, out, near, route, gain, held,
    queries, keys, values, done, gain_done, held_done,
):
    rows, width = queries.shape
    group = width // GROUPS
    copies = []
    for h in range(GROUPS):
        columns = slice(group * h, group * (h + 1))
        pairs = ((queries_hbm, queries), (keys_hbm, keys), (values_hbm, values))
        copies.append(
            [
                pltpu.make_async_copy(source.at[:, columns], held.at[:, columns], done.at[i, h])
                for i, (source, held) in enumerate(pairs)
            ]
        )
        for copy in copies[h]:
            copy.start()
    gain_copy = pltpu.make_async_copy(gain_hbm, gain, gain_done)
    gain_copy.start()
    fetches = column_copies(weight, held, held_done, ((2, 0),))

    def flag(k, first):
        after = first + CH * counts[k]
        reset = jnp.int32(0)
        for b in range(SESSIONS):
            reset = reset | ((starts[b] >= first) & (starts[b] < after)).astype(jnp.int32)
        near[k] = reset
        return after

    lax.fori_loop(0, counts.shape[0], flag, jnp.int32(0))

    def note(j, carry):
        route[j] = device[j]
        return carry

    lax.fori_loop(0, device.shape[0], note, 0)
    row = lax.broadcasted_iota(jnp.int32, (rows, 1), 0)
    lower = jnp.full((rows, 1), -FAR, jnp.int32)
    for b in range(SESSIONS):
        lower = jnp.maximum(lower, jnp.where(row >= info[3 + b], info[3 + b], -FAR))
    column = lax.broadcasted_iota(jnp.int32, (rows, rows), 1)
    allowed = (column <= row) & (column >= lower)
    for h in range(width // DH):
        columns = slice(DH * h, DH * (h + 1))
        if DH * h % group == 0:
            for copy in copies[DH * h // group]:
                copy.wait()
        phi_q = feature(queries[:, columns])
        phi_k = feature(keys[:, columns])
        phi_out[:, columns] = phi_q
        scores = lax.dot_general(
            phi_q, phi_k, (((1,), (1,)), ((), ())), preferred_element_type=jnp.float32
        )
        scores = jnp.where(allowed, scores, 0.0).astype(jnp.bfloat16)
        out[:, columns] = jnp.dot(
            scores, values[:, columns], preferred_element_type=jnp.float32
        ).astype(jnp.bfloat16)
    gain_copy.wait()
    for fetch in fetches:
        fetch.wait()


def attend_kernel(
    info, device, phi_q, inside, state, gain, weight, out, held, scratch, done
):
    fetches = column_copies(weight, held, done, ((2, 1),))
    rows, width = phi_q.shape
    row = lax.broadcasted_iota(jnp.int32, (rows, 1), 0)
    open_row = row < info[2]
    for h in range(width // DH):
        columns = slice(DH * h, DH * (h + 1))
        carried = jnp.dot(phi_q[:, columns], state[h], preferred_element_type=jnp.float32)
        numer = inside[:, columns].astype(jnp.float32) + jnp.where(open_row, carried, 0.0)
        inverse = lax.rsqrt(jnp.mean(numer * numer, axis=1, keepdims=True) + EPSILON)
        scratch[:, columns] = numer * inverse * gain[:, columns]

    def place(j, carry):
        start = pl.multiple_of(j * CH, CH)
        out[device[j]] = scratch[pl.ds(start, CH), :].astype(jnp.bfloat16)
        return carry

    lax.fori_loop(0, info[7], place, 0)
    for fetch in fetches:
        fetch.wait()


def product(packed, weight, out):
    out[...] = jnp.dot(packed[...], weight, preferred_element_type=jnp.float32).astype(
        jnp.bfloat16
    )


def across_kernel(slots, arrived, for_left, for_right, packed, left, right, source):
    for s in range(arrived.shape[0]):
        slot = slots[0, s]
        source[jnp.where(slot < 0, BAL, slot)] = jnp.int32(s)
    for i in range(0, BAL, 2):
        packed[CH * i : CH * (i + 2), :] = jnp.concatenate(
            [arrived[source[i]], arrived[source[i + 1]]], axis=0
        )
    product(packed, for_left[0], left)
    product(packed, for_right[0], right)


def beside_kernel(packed, weight, ahead_right, behind_left, later, held, later_done, done):
    last = lax.axis_size("head") - 1
    copies = column_copies(weight, held, done, ((1, 1), (last, 0)))
    fetches = column_copies(weight, later, later_done, ((1, 0), (last, 1)))
    for n, out in enumerate((ahead_right, behind_left)):
        copies[n].wait()
        product(packed, held[n], out)
    for fetch in fetches:
        fetch.wait()


def join_kernel(packed, kept, up, down, left, right):
    for n, (arrived, out) in enumerate(((up, left), (down, right))):
        own = jnp.dot(packed[...], kept[n], preferred_element_type=jnp.float32)
        own = own.astype(jnp.bfloat16).astype(jnp.float32)
        out[...] = (own + arrived[...].astype(jnp.float32)).astype(jnp.bfloat16)


def own_kernel(packed, weight, from_ahead, from_behind, left, right, held, done):
    copies = column_copies(weight, held, done, ((0, 0), (0, 1)))
    for n, (arrived, out) in enumerate(((from_ahead, left), (from_behind, right))):
        copies[n].wait()
        own = jnp.dot(packed[...], held[n], preferred_element_type=jnp.float32)
        own = own.astype(jnp.bfloat16).astype(jnp.float32)
        out[...] = own + arrived[...].astype(jnp.float32)


def ctx_exchange(x):
    return lax.all_to_all(x, "ctx", split_axis=0, concat_axis=0, tiled=True)


def head_shift(x, by):
    count = lax.axis_size("head")
    return lax.ppermute(x, "head", [(i, (i + by) % count) for i in range(count)])


def wide(x):
    return x.astype(jnp.float32)


def per_device(
    queries,
    keys,
    values,
    out_weight,
    norm_gain,
    tile_counts,
    route_device,
    route_slot,
    session_starts,
):
    ranks = lax.axis_size("ctx")
    groups = lax.axis_size("head")
    rows, width = queries.shape
    heads = width // DH
    part = heads * DH // ranks
    smem = pl.BlockSpec(memory_space=SMEM)
    vmem = pl.BlockSpec(memory_space=VMEM)
    hbm = pl.BlockSpec(memory_space=HBM)
    in_hbm = lambda x: pltpu.with_memory_space_constraint(x, HBM)
    params = pltpu.CompilerParams(vmem_limit_bytes=16 << 20)

    tables = [in_hbm(x) for x in (tile_counts, session_starts, route_device, route_slot)]
    tile_counts, session_starts, route_device, route_slot = tables
    entry, info = pl.pallas_call(
        entry_kernel,
        in_specs=[hbm] * 6,
        out_specs=[vmem, smem],
        out_shape=[
            jax.ShapeDtypeStruct((ranks, part // 2 + 1, 2, DH), jnp.bfloat16),
            jax.ShapeDtypeStruct((8,), jnp.int32),
        ],
        scratch_shapes=[
            pltpu.VMEM((rows, width), keys.dtype),
            pltpu.VMEM((rows, width), values.dtype),
            *[pltpu.SMEM(x.shape, jnp.int32) for x in tables],
            pltpu.SemaphoreType.DMA((2, GROUPS)),
            pltpu.SemaphoreType.DMA((4,)),
        ],
        compiler_params=params,
        name="entry",
    )(*tables, in_hbm(keys), in_hbm(values))

    got = ctx_exchange(entry)

    half = out_weight.shape[1] // groups // 2
    held = lambda n: jax.ShapeDtypeStruct((n, width, half), out_weight.dtype)
    phi_q, inside, resets, route, gain, for_left = pl.pallas_call(
        inside_kernel,
        in_specs=[smem] * 4 + [hbm] * 5,
        out_specs=[vmem] * 2 + [smem] * 2 + [vmem] * 2,
        out_shape=[
            jax.ShapeDtypeStruct((rows, width), jnp.bfloat16),
            jax.ShapeDtypeStruct((rows, width), jnp.bfloat16),
            jax.ShapeDtypeStruct(tile_counts.shape, jnp.int32),
            jax.ShapeDtypeStruct(route_device.shape, jnp.int32),
            jax.ShapeDtypeStruct((1, width), jnp.float32),
            held(1),
        ],
        scratch_shapes=[
            *[pltpu.VMEM((rows, width), jnp.bfloat16)] * 3,
            pltpu.SemaphoreType.DMA((3, GROUPS)),
            pltpu.SemaphoreType.DMA,
            pltpu.SemaphoreType.DMA((1,)),
        ],
        compiler_params=params,
        name="inside",
    )(
        info,
        tile_counts,
        session_starts,
        route_device,
        in_hbm(norm_gain.reshape(1, width)),
        in_hbm(queries),
        in_hbm(keys),
        in_hbm(values),
        in_hbm(out_weight),
    )

    got, phi_q, inside, resets = lax.optimization_barrier((got, phi_q, inside, resets))
    summed, slots = pl.pallas_call(
        prefix_kernel,
        in_specs=[smem, vmem],
        out_specs=[vmem] * 2,
        out_shape=[
            jax.ShapeDtypeStruct((ranks, part, DH), jnp.bfloat16),
            jax.ShapeDtypeStruct((1, DH), jnp.int32),
        ],
        compiler_params=params,
        name="prefix",
    )(resets, got)

    state = ctx_exchange(summed).reshape(heads, DH, DH)

    payload, for_right = pl.pallas_call(
        attend_kernel,
        in_specs=[smem] * 2 + [vmem] * 4 + [hbm],
        out_specs=[vmem] * 2,
        out_shape=[jax.ShapeDtypeStruct((ranks, CH, width), jnp.bfloat16), held(1)],
        scratch_shapes=[pltpu.VMEM((rows, width), jnp.float32), pltpu.SemaphoreType.DMA((1,))],
        compiler_params=params,
        name="attend",
    )(info, route, phi_q, inside, state, gain, in_hbm(out_weight))

    arrived = ctx_exchange(payload)

    piece = jax.ShapeDtypeStruct((BAL * CH, half), jnp.bfloat16)
    packed, *across = pl.pallas_call(
        across_kernel,
        in_specs=[smem] + [vmem] * 3,
        out_specs=[vmem] * 3,
        out_shape=[jax.ShapeDtypeStruct((BAL * CH, width), jnp.bfloat16), piece, piece],
        scratch_shapes=[pltpu.SMEM((BAL + 1,), jnp.int32)],
        compiler_params=params,
        name="across",
    )(slots, arrived, for_left, for_right)
    up = head_shift(across[0], 1)
    down = head_shift(across[1], -1)

    ahead_right, behind_left, later = pl.pallas_call(
        beside_kernel,
        in_specs=[vmem, hbm],
        out_specs=[vmem] * 3,
        out_shape=[piece, piece, held(2)],
        scratch_shapes=[
            pltpu.VMEM((2, width, half), out_weight.dtype),
            pltpu.SemaphoreType.DMA((2,)),
            pltpu.SemaphoreType.DMA((2,)),
        ],
        compiler_params=params,
        name="beside",
    )(packed, in_hbm(out_weight))
    from_behind = head_shift(ahead_right, 1)
    from_ahead = head_shift(behind_left, -1)

    left_sum, right_sum = pl.pallas_call(
        join_kernel,
        in_specs=[vmem] * 4,
        out_specs=[vmem] * 2,
        out_shape=[piece] * 2,
        compiler_params=params,
        name="join",
    )(packed, later, up, down)
    last_left = head_shift(left_sum, 1)
    last_right = head_shift(right_sum, -1)

    left, right = pl.pallas_call(
        own_kernel,
        in_specs=[vmem, hbm, vmem, vmem],
        out_specs=[vmem] * 2,
        out_shape=[jax.ShapeDtypeStruct((BAL * CH, half), jnp.float32)] * 2,
        scratch_shapes=[
            pltpu.VMEM((2, width, half), out_weight.dtype),
            pltpu.SemaphoreType.DMA((2,)),
        ],
        compiler_params=params,
        name="own",
    )(packed, in_hbm(out_weight), from_ahead, from_behind)
    left = left + wide(last_left)
    right = right + wide(last_right)
    return jnp.concatenate([left, right], axis=1).astype(jnp.bfloat16)


def solution(mesh):
    placed = (
        P("ctx", "head"),
        P("ctx", "head"),
        P("ctx", "head"),
        P("head", None),
        P("head"),
        P(),
        P("ctx"),
        P("ctx"),
        P(),
    )
    return jax.shard_map(
        per_device, mesh=mesh, in_specs=placed, out_specs=P("ctx", "head"), check_vma=False
    )
```

```python
import jax
import jax.numpy as jnp
from jax import lax
from jax.experimental import pallas as pl
from jax.experimental.pallas import tpu as pltpu
from jax.sharding import PartitionSpec as P

DH = 128
CH = 8
BAL = 32
SESSIONS = 4
GROUPS = 2
EPSILON = 1e-06
FAR = 1 << 28
SMEM = pltpu.MemorySpace.SMEM
VMEM = pltpu.MemorySpace.VMEM
HBM = pltpu.MemorySpace.HBM


def feature(block):
    value = block.astype(jnp.float32)
    return jnp.where(value > 0, value + 1.0, jnp.exp(jnp.minimum(value, 0.0))).astype(jnp.bfloat16)


def entry_kernel(
    counts_hbm, starts_hbm, device_hbm, slot_hbm, keys_hbm, values_hbm,
    out, info, keys, values, counts, starts, device, slot, done, small,
):
    ranks = counts.shape[0]
    here = lax.axis_index("ctx")
    rows, width = keys.shape
    part = width // ranks
    tables = ((counts_hbm, counts), (starts_hbm, starts), (device_hbm, device), (slot_hbm, slot))
    tables = [pltpu.make_async_copy(a, b, small.at[i]) for i, (a, b) in enumerate(tables)]
    for copy in tables:
        copy.start()
    copies = []
    for h in range(GROUPS):
        columns = slice(width // GROUPS * h, width // GROUPS * (h + 1))
        pair = [
            pltpu.make_async_copy(source.at[:, columns], held.at[:, columns], done.at[i, h])
            for i, (source, held) in enumerate(((keys_hbm, keys), (values_hbm, values)))
        ]
        copies.append(pair)
        for copy in pair:
            copy.start()
    for copy in tables:
        copy.wait()

    def add(k, total):
        return total + jnp.where(k < here, counts[k], 0)

    offset = CH * lax.fori_loop(0, ranks, add, jnp.int32(0), unroll=8)
    live = CH * counts[here]
    last_start = jnp.int32(-FAR)
    next_start = jnp.int32(FAR)
    for b in range(SESSIONS):
        local = starts[b] - offset
        info[3 + b] = local
        last_start = jnp.maximum(last_start, jnp.where(local <= live - 1, local, -FAR))
        next_start = jnp.minimum(next_start, jnp.where(local >= 0, local, FAR))
    info[0] = last_start
    info[1] = live
    info[2] = next_start
    info[7] = counts[here]

    out[:, part // 2 :] = jnp.full((ranks, 1, 2, DH), -1.0, jnp.bfloat16)

    def mark(j, carry):
        value = jnp.full((1, 2, DH), slot[j], jnp.int32)
        out[device[j], part // 2 :] = value.astype(jnp.float32).astype(jnp.bfloat16)
        return carry

    lax.fori_loop(0, counts[here], mark, 0)

    row = lax.broadcasted_iota(jnp.int32, (rows, DH), 0)
    kept = (row >= last_start) & (row < live)
    each = DH // part
    for h in range(width // DH):
        columns = slice(DH * h, DH * (h + 1))
        if h % (width // DH // GROUPS) == 0:
            for copy in copies[h // (width // DH // GROUPS)]:
                copy.wait()
        phi = jnp.where(kept, feature(keys[:, columns]).astype(jnp.float32), 0.0)
        state = lax.dot_general(
            phi.astype(jnp.bfloat16),
            values[:, columns],
            (((0,), (0,)), ((), ())),
            preferred_element_type=jnp.float32,
        ).astype(jnp.bfloat16)
        for i in range(each):
            out[each * h + i, : part // 2] = state[part * i : part * (i + 1), :].reshape(part // 2, 2, DH)


def column_copies(weight, held, done, pieces):
    groups = lax.axis_size("head")
    block = weight.shape[1] // groups
    half = block // 2
    copies = []
    for n, (by, i) in enumerate(pieces):
        column = lax.rem(lax.axis_index("head") + by, groups)
        start = pl.multiple_of(column * block + i * half, half)
        copies.append(
            pltpu.make_async_copy(weight.at[:, pl.ds(start, half)], held.at[n], done.at[n])
        )
    for copy in copies:
        copy.start()
    return copies


def prefix_kernel(flags, got, weight, out, slots, held, resets, done, held_done):
    fetches = column_copies(weight, held, held_done, ((2, 1),))
    flag_copy = pltpu.make_async_copy(flags, resets, done)
    flag_copy.start()
    ranks, part, _ = out.shape
    lane = lax.broadcasted_iota(jnp.int32, (2, DH), 1)
    gathered = jnp.zeros((2, DH), jnp.float32)
    for k in range(ranks):
        gathered = jnp.where(lane == k, got[k, part // 2].astype(jnp.float32), gathered)
    slots[...] = gathered[:1].astype(jnp.int32)
    flag_copy.wait()
    running = jnp.zeros((part, DH), jnp.float32)
    for k in range(ranks):
        out[k] = running.astype(jnp.bfloat16)
        if k + 1 < ranks:
            keep = jnp.full((part, DH), 1 - resets[k], jnp.int32) > 0
            entry = got[k, : part // 2].reshape(part, DH).astype(jnp.float32)
            running = jnp.where(keep, running, 0.0) + entry
    for fetch in fetches:
        fetch.wait()


def inside_kernel(
    info, counts, starts, device, gain_hbm, queries_hbm, keys_hbm, values_hbm, weight,
    phi_out, out, near, route, gain, held,
    queries, keys, values, done, gain_done, held_done,
):
    rows, width = queries.shape
    group = width // GROUPS
    copies = []
    for h in range(GROUPS):
        columns = slice(group * h, group * (h + 1))
        pairs = ((queries_hbm, queries), (keys_hbm, keys), (values_hbm, values))
        copies.append(
            [
                pltpu.make_async_copy(source.at[:, columns], held.at[:, columns], done.at[i, h])
                for i, (source, held) in enumerate(pairs)
            ]
        )
        for copy in copies[h]:
            copy.start()
    gain_copy = pltpu.make_async_copy(gain_hbm, gain, gain_done)
    gain_copy.start()
    fetches = column_copies(weight, held, held_done, ((2, 0),))

    def flag(k, first):
        after = first + CH * counts[k]
        reset = jnp.int32(0)
        for b in range(SESSIONS):
            reset = reset | ((starts[b] >= first) & (starts[b] < after)).astype(jnp.int32)
        near[k] = reset
        return after

    lax.fori_loop(0, counts.shape[0], flag, jnp.int32(0))

    def note(j, carry):
        route[j] = device[j]
        return carry

    lax.fori_loop(0, device.shape[0], note, 0)
    row = lax.broadcasted_iota(jnp.int32, (rows, 1), 0)
    lower = jnp.full((rows, 1), -FAR, jnp.int32)
    for b in range(SESSIONS):
        lower = jnp.maximum(lower, jnp.where(row >= info[3 + b], info[3 + b], -FAR))
    column = lax.broadcasted_iota(jnp.int32, (rows, rows), 1)
    allowed = (column <= row) & (column >= lower)
    for h in range(width // DH):
        columns = slice(DH * h, DH * (h + 1))
        if DH * h % group == 0:
            for copy in copies[DH * h // group]:
                copy.wait()
        phi_q = feature(queries[:, columns])
        phi_k = feature(keys[:, columns])
        phi_out[:, columns] = phi_q
        scores = lax.dot_general(
            phi_q, phi_k, (((1,), (1,)), ((), ())), preferred_element_type=jnp.float32
        )
        scores = jnp.where(allowed, scores, 0.0).astype(jnp.bfloat16)
        out[:, columns] = jnp.dot(
            scores, values[:, columns], preferred_element_type=jnp.float32
        ).astype(jnp.bfloat16)
    gain_copy.wait()
    for fetch in fetches:
        fetch.wait()


def attend_kernel(
    info, device, phi_q, inside, state, gain, out, scratch
):
    rows, width = phi_q.shape
    row = lax.broadcasted_iota(jnp.int32, (rows, 1), 0)
    open_row = row < info[2]
    for h in range(width // DH):
        columns = slice(DH * h, DH * (h + 1))
        carried = jnp.dot(phi_q[:, columns], state[h], preferred_element_type=jnp.float32)
        numer = inside[:, columns].astype(jnp.float32) + jnp.where(open_row, carried, 0.0)
        inverse = lax.rsqrt(jnp.mean(numer * numer, axis=1, keepdims=True) + EPSILON)
        scratch[:, columns] = numer * inverse * gain[:, columns]

    def place(j, carry):
        start = pl.multiple_of(j * CH, CH)
        out[device[j]] = scratch[pl.ds(start, CH), :].astype(jnp.bfloat16)
        return carry

    lax.fori_loop(0, info[7], place, 0)


def product(packed, weight, out):
    out[...] = jnp.dot(packed[...], weight, preferred_element_type=jnp.float32).astype(
        jnp.bfloat16
    )


def across_kernel(slots, arrived, for_left, for_right, packed, left, right, source):
    for s in range(arrived.shape[0]):
        slot = slots[0, s]
        source[jnp.where(slot < 0, BAL, slot)] = jnp.int32(s)
    for i in range(0, BAL, 2):
        packed[CH * i : CH * (i + 2), :] = jnp.concatenate(
            [arrived[source[i]], arrived[source[i + 1]]], axis=0
        )
    product(packed, for_left[0], left)
    product(packed, for_right[0], right)


def beside_kernel(packed, weight, ahead_right, behind_left, later, held, later_done, done):
    last = lax.axis_size("head") - 1
    copies = column_copies(weight, held, done, ((1, 1), (last, 0)))
    fetches = column_copies(weight, later, later_done, ((1, 0), (last, 1)))
    for n, out in enumerate((ahead_right, behind_left)):
        copies[n].wait()
        product(packed, held[n], out)
    for fetch in fetches:
        fetch.wait()


def join_kernel(packed, kept, up, down, left, right):
    for n, (arrived, out) in enumerate(((up, left), (down, right))):
        own = jnp.dot(packed[...], kept[n], preferred_element_type=jnp.float32)
        own = own.astype(jnp.bfloat16).astype(jnp.float32)
        out[...] = (own + arrived[...].astype(jnp.float32)).astype(jnp.bfloat16)


def own_kernel(packed, weight, from_ahead, from_behind, left, right, held, done):
    copies = column_copies(weight, held, done, ((0, 0), (0, 1)))
    for n, (arrived, out) in enumerate(((from_ahead, left), (from_behind, right))):
        copies[n].wait()
        own = jnp.dot(packed[...], held[n], preferred_element_type=jnp.float32)
        own = own.astype(jnp.bfloat16).astype(jnp.float32)
        out[...] = own + arrived[...].astype(jnp.float32)


def ctx_exchange(x):
    return lax.all_to_all(x, "ctx", split_axis=0, concat_axis=0, tiled=True)


def head_shift(x, by):
    count = lax.axis_size("head")
    return lax.ppermute(x, "head", [(i, (i + by) % count) for i in range(count)])


def wide(x):
    return x.astype(jnp.float32)


def per_device(
    queries,
    keys,
    values,
    out_weight,
    norm_gain,
    tile_counts,
    route_device,
    route_slot,
    session_starts,
):
    ranks = lax.axis_size("ctx")
    groups = lax.axis_size("head")
    rows, width = queries.shape
    heads = width // DH
    part = heads * DH // ranks
    smem = pl.BlockSpec(memory_space=SMEM)
    vmem = pl.BlockSpec(memory_space=VMEM)
    hbm = pl.BlockSpec(memory_space=HBM)
    in_hbm = lambda x: pltpu.with_memory_space_constraint(x, HBM)
    params = pltpu.CompilerParams(vmem_limit_bytes=16 << 20)

    tables = [in_hbm(x) for x in (tile_counts, session_starts, route_device, route_slot)]
    tile_counts, session_starts, route_device, route_slot = tables
    entry, info = pl.pallas_call(
        entry_kernel,
        in_specs=[hbm] * 6,
        out_specs=[vmem, smem],
        out_shape=[
            jax.ShapeDtypeStruct((ranks, part // 2 + 1, 2, DH), jnp.bfloat16),
            jax.ShapeDtypeStruct((8,), jnp.int32),
        ],
        scratch_shapes=[
            pltpu.VMEM((rows, width), keys.dtype),
            pltpu.VMEM((rows, width), values.dtype),
            *[pltpu.SMEM(x.shape, jnp.int32) for x in tables],
            pltpu.SemaphoreType.DMA((2, GROUPS)),
            pltpu.SemaphoreType.DMA((4,)),
        ],
        compiler_params=params,
        name="entry",
    )(*tables, in_hbm(keys), in_hbm(values))

    got = ctx_exchange(entry)

    half = out_weight.shape[1] // groups // 2
    held = lambda n: jax.ShapeDtypeStruct((n, width, half), out_weight.dtype)
    phi_q, inside, resets, route, gain, for_left = pl.pallas_call(
        inside_kernel,
        in_specs=[smem] * 4 + [hbm] * 5,
        out_specs=[vmem] * 2 + [smem] * 2 + [vmem] * 2,
        out_shape=[
            jax.ShapeDtypeStruct((rows, width), jnp.bfloat16),
            jax.ShapeDtypeStruct((rows, width), jnp.bfloat16),
            jax.ShapeDtypeStruct(tile_counts.shape, jnp.int32),
            jax.ShapeDtypeStruct(route_device.shape, jnp.int32),
            jax.ShapeDtypeStruct((1, width), jnp.float32),
            held(1),
        ],
        scratch_shapes=[
            *[pltpu.VMEM((rows, width), jnp.bfloat16)] * 3,
            pltpu.SemaphoreType.DMA((3, GROUPS)),
            pltpu.SemaphoreType.DMA,
            pltpu.SemaphoreType.DMA((1,)),
        ],
        compiler_params=params,
        name="inside",
    )(
        info,
        tile_counts,
        session_starts,
        route_device,
        in_hbm(norm_gain.reshape(1, width)),
        in_hbm(queries),
        in_hbm(keys),
        in_hbm(values),
        in_hbm(out_weight),
    )

    got, phi_q, inside, resets = lax.optimization_barrier((got, phi_q, inside, resets))
    summed, slots, for_right = pl.pallas_call(
        prefix_kernel,
        in_specs=[vmem, vmem, hbm],
        out_specs=[vmem] * 3,
        out_shape=[
            jax.ShapeDtypeStruct((ranks, part, DH), jnp.bfloat16),
            jax.ShapeDtypeStruct((1, DH), jnp.int32),
            held(1),
        ],
        scratch_shapes=[
            pltpu.SMEM(tile_counts.shape, jnp.int32),
            pltpu.SemaphoreType.DMA,
            pltpu.SemaphoreType.DMA((1,)),
        ],
        compiler_params=params,
        name="prefix",
    )(resets, got, in_hbm(out_weight))

    state = ctx_exchange(summed).reshape(heads, DH, DH)

    payload = pl.pallas_call(
        attend_kernel,
        in_specs=[smem] * 2 + [vmem] * 4,
        out_specs=vmem,
        out_shape=jax.ShapeDtypeStruct((ranks, CH, width), jnp.bfloat16),
        scratch_shapes=[pltpu.VMEM((rows, width), jnp.float32)],
        compiler_params=params,
        name="attend",
    )(info, route, phi_q, inside, state, gain)

    arrived = ctx_exchange(payload)

    piece = jax.ShapeDtypeStruct((BAL * CH, half), jnp.bfloat16)
    packed, *across = pl.pallas_call(
        across_kernel,
        in_specs=[smem] + [vmem] * 3,
        out_specs=[vmem] * 3,
        out_shape=[jax.ShapeDtypeStruct((BAL * CH, width), jnp.bfloat16), piece, piece],
        scratch_shapes=[pltpu.SMEM((BAL + 1,), jnp.int32)],
        compiler_params=params,
        name="across",
    )(slots, arrived, for_left, for_right)
    up = head_shift(across[0], 1)
    down = head_shift(across[1], -1)

    ahead_right, behind_left, later = pl.pallas_call(
        beside_kernel,
        in_specs=[vmem, hbm],
        out_specs=[vmem] * 3,
        out_shape=[piece, piece, held(2)],
        scratch_shapes=[
            pltpu.VMEM((2, width, half), out_weight.dtype),
            pltpu.SemaphoreType.DMA((2,)),
            pltpu.SemaphoreType.DMA((2,)),
        ],
        compiler_params=params,
        name="beside",
    )(packed, in_hbm(out_weight))
    from_behind = head_shift(ahead_right, 1)
    from_ahead = head_shift(behind_left, -1)

    left_sum, right_sum = pl.pallas_call(
        join_kernel,
        in_specs=[vmem] * 4,
        out_specs=[vmem] * 2,
        out_shape=[piece] * 2,
        compiler_params=params,
        name="join",
    )(packed, later, up, down)
    last_left = head_shift(left_sum, 1)
    last_right = head_shift(right_sum, -1)

    left, right = pl.pallas_call(
        own_kernel,
        in_specs=[vmem, hbm, vmem, vmem],
        out_specs=[vmem] * 2,
        out_shape=[jax.ShapeDtypeStruct((BAL * CH, half), jnp.float32)] * 2,
        scratch_shapes=[
            pltpu.VMEM((2, width, half), out_weight.dtype),
            pltpu.SemaphoreType.DMA((2,)),
        ],
        compiler_params=params,
        name="own",
    )(packed, in_hbm(out_weight), from_ahead, from_behind)
    left = left + wide(last_left)
    right = right + wide(last_right)
    return jnp.concatenate([left, right], axis=1).astype(jnp.bfloat16)


def solution(mesh):
    placed = (
        P("ctx", "head"),
        P("ctx", "head"),
        P("ctx", "head"),
        P("head", None),
        P("head"),
        P(),
        P("ctx"),
        P("ctx"),
        P(),
    )
    return jax.shard_map(
        per_device, mesh=mesh, in_specs=placed, out_specs=P("ctx", "head"), check_vma=False
    )
```

```python
import jax
import jax.numpy as jnp
from jax import lax
from jax.experimental import pallas as pl
from jax.experimental.pallas import tpu as pltpu
from jax.sharding import PartitionSpec as P

DH = 128
CH = 8
BAL = 32
SESSIONS = 4
GROUPS = 2
EPSILON = 1e-06
FAR = 1 << 28
SMEM = pltpu.MemorySpace.SMEM
VMEM = pltpu.MemorySpace.VMEM
HBM = pltpu.MemorySpace.HBM


def feature(block):
    value = block.astype(jnp.float32)
    return jnp.where(value > 0, value + 1.0, jnp.exp(jnp.minimum(value, 0.0))).astype(jnp.bfloat16)


def entry_kernel(
    counts_hbm, starts_hbm, device_hbm, slot_hbm, keys_hbm, values_hbm,
    out, info, keys, values, counts, starts, device, slot, done, small,
):
    ranks = counts.shape[0]
    here = lax.axis_index("ctx")
    rows, width = keys.shape
    part = width // ranks
    tables = ((counts_hbm, counts), (starts_hbm, starts), (device_hbm, device), (slot_hbm, slot))
    tables = [pltpu.make_async_copy(a, b, small.at[i]) for i, (a, b) in enumerate(tables)]
    for copy in tables:
        copy.start()
    copies = []
    for h in range(GROUPS):
        columns = slice(width // GROUPS * h, width // GROUPS * (h + 1))
        pair = [
            pltpu.make_async_copy(source.at[:, columns], held.at[:, columns], done.at[i, h])
            for i, (source, held) in enumerate(((keys_hbm, keys), (values_hbm, values)))
        ]
        copies.append(pair)
        for copy in pair:
            copy.start()
    for copy in tables:
        copy.wait()

    def add(k, total):
        return total + jnp.where(k < here, counts[k], 0)

    offset = CH * lax.fori_loop(0, ranks, add, jnp.int32(0), unroll=8)
    live = CH * counts[here]
    last_start = jnp.int32(-FAR)
    next_start = jnp.int32(FAR)
    for b in range(SESSIONS):
        local = starts[b] - offset
        info[3 + b] = local
        last_start = jnp.maximum(last_start, jnp.where(local <= live - 1, local, -FAR))
        next_start = jnp.minimum(next_start, jnp.where(local >= 0, local, FAR))
    info[0] = last_start
    info[1] = live
    info[2] = next_start
    info[7] = counts[here]

    out[:, part // 2 :] = jnp.full((ranks, 1, 2, DH), -1.0, jnp.bfloat16)

    def mark(j, carry):
        value = jnp.full((1, 2, DH), slot[j], jnp.int32)
        out[device[j], part // 2 :] = value.astype(jnp.float32).astype(jnp.bfloat16)
        return carry

    lax.fori_loop(0, counts[here], mark, 0)

    row = lax.broadcasted_iota(jnp.int32, (rows, DH), 0)
    kept = (row >= last_start) & (row < live)
    each = DH // part
    for h in range(width // DH):
        columns = slice(DH * h, DH * (h + 1))
        if h % (width // DH // GROUPS) == 0:
            for copy in copies[h // (width // DH // GROUPS)]:
                copy.wait()
        phi = jnp.where(kept, feature(keys[:, columns]).astype(jnp.float32), 0.0)
        state = lax.dot_general(
            phi.astype(jnp.bfloat16),
            values[:, columns],
            (((0,), (0,)), ((), ())),
            preferred_element_type=jnp.float32,
        ).astype(jnp.bfloat16)
        for i in range(each):
            out[each * h + i, : part // 2] = state[part * i : part * (i + 1), :].reshape(part // 2, 2, DH)


def column_copies(weight, held, done, pieces):
    groups = lax.axis_size("head")
    block = weight.shape[1] // groups
    half = block // 2
    copies = []
    for n, (by, i) in enumerate(pieces):
        column = lax.rem(lax.axis_index("head") + by, groups)
        start = pl.multiple_of(column * block + i * half, half)
        copies.append(
            pltpu.make_async_copy(weight.at[:, pl.ds(start, half)], held.at[n], done.at[n])
        )
    for copy in copies:
        copy.start()
    return copies


def prefix_kernel(flags, got, weight, out, slots, held, resets, done, held_done):
    fetches = column_copies(weight, held, held_done, ((2, 1),))
    flag_copy = pltpu.make_async_copy(flags, resets, done)
    flag_copy.start()
    ranks, pairs = out.shape[:2]
    part = 2 * pairs
    lane = lax.broadcasted_iota(jnp.int32, (2, DH), 1)
    gathered = jnp.zeros((2, DH), jnp.float32)
    for k in range(ranks):
        gathered = jnp.where(lane == k, got[k, part // 2].astype(jnp.float32), gathered)
    slots[...] = gathered[:1].astype(jnp.int32)
    flag_copy.wait()
    running = jnp.zeros((part, DH), jnp.float32)
    for k in range(ranks):
        out[k] = running.astype(jnp.bfloat16).reshape(pairs, 2, DH)
        if k + 1 < ranks:
            keep = jnp.full((part, DH), 1 - resets[k], jnp.int32) > 0
            entry = got[k, : part // 2].reshape(part, DH).astype(jnp.float32)
            running = jnp.where(keep, running, 0.0) + entry
    for fetch in fetches:
        fetch.wait()


def inside_kernel(
    info, counts, starts, device, gain_hbm, queries_hbm, keys_hbm, values_hbm, weight,
    phi_out, out, near, route, gain, held,
    queries, keys, values, done, gain_done, held_done,
):
    rows, width = queries.shape
    group = width // GROUPS
    copies = []
    for h in range(GROUPS):
        columns = slice(group * h, group * (h + 1))
        pairs = ((queries_hbm, queries), (keys_hbm, keys), (values_hbm, values))
        copies.append(
            [
                pltpu.make_async_copy(source.at[:, columns], held.at[:, columns], done.at[i, h])
                for i, (source, held) in enumerate(pairs)
            ]
        )
        for copy in copies[h]:
            copy.start()
    gain_copy = pltpu.make_async_copy(gain_hbm, gain, gain_done)
    gain_copy.start()
    fetches = column_copies(weight, held, held_done, ((2, 0),))

    def flag(k, first):
        after = first + CH * counts[k]
        reset = jnp.int32(0)
        for b in range(SESSIONS):
            reset = reset | ((starts[b] >= first) & (starts[b] < after)).astype(jnp.int32)
        near[k] = reset
        return after

    lax.fori_loop(0, counts.shape[0], flag, jnp.int32(0))

    def note(j, carry):
        route[j] = device[j]
        return carry

    lax.fori_loop(0, device.shape[0], note, 0)
    row = lax.broadcasted_iota(jnp.int32, (rows, 1), 0)
    lower = jnp.full((rows, 1), -FAR, jnp.int32)
    for b in range(SESSIONS):
        lower = jnp.maximum(lower, jnp.where(row >= info[3 + b], info[3 + b], -FAR))
    column = lax.broadcasted_iota(jnp.int32, (rows, rows), 1)
    allowed = (column <= row) & (column >= lower)
    for h in range(width // DH):
        columns = slice(DH * h, DH * (h + 1))
        if DH * h % group == 0:
            for copy in copies[DH * h // group]:
                copy.wait()
        phi_q = feature(queries[:, columns])
        phi_k = feature(keys[:, columns])
        phi_out[:, columns] = phi_q
        scores = lax.dot_general(
            phi_q, phi_k, (((1,), (1,)), ((), ())), preferred_element_type=jnp.float32
        )
        scores = jnp.where(allowed, scores, 0.0).astype(jnp.bfloat16)
        out[:, columns] = jnp.dot(
            scores, values[:, columns], preferred_element_type=jnp.float32
        ).astype(jnp.bfloat16)
    gain_copy.wait()
    for fetch in fetches:
        fetch.wait()


def attend_kernel(
    info, device, phi_q, inside, state, gain, out, scratch
):
    rows, width = phi_q.shape
    row = lax.broadcasted_iota(jnp.int32, (rows, 1), 0)
    open_row = row < info[2]
    for h in range(width // DH):
        columns = slice(DH * h, DH * (h + 1))
        carried = jnp.dot(phi_q[:, columns], state[h], preferred_element_type=jnp.float32)
        numer = inside[:, columns].astype(jnp.float32) + jnp.where(open_row, carried, 0.0)
        inverse = lax.rsqrt(jnp.mean(numer * numer, axis=1, keepdims=True) + EPSILON)
        scratch[:, columns] = numer * inverse * gain[:, columns]

    def place(j, carry):
        start = pl.multiple_of(j * CH, CH)
        out[device[j]] = scratch[pl.ds(start, CH), :].astype(jnp.bfloat16)
        return carry

    lax.fori_loop(0, info[7], place, 0)


def product(packed, weight, out):
    out[...] = jnp.dot(packed[...], weight, preferred_element_type=jnp.float32).astype(
        jnp.bfloat16
    )


def across_kernel(slots, arrived, for_left, for_right, packed, left, right, source):
    for s in range(arrived.shape[0]):
        slot = slots[0, s]
        source[jnp.where(slot < 0, BAL, slot)] = jnp.int32(s)
    for i in range(0, BAL, 2):
        packed[CH * i : CH * (i + 2), :] = jnp.concatenate(
            [arrived[source[i]], arrived[source[i + 1]]], axis=0
        )
    product(packed, for_left[0], left)
    product(packed, for_right[0], right)


def beside_kernel(packed, weight, ahead_right, behind_left, later, held, later_done, done):
    last = lax.axis_size("head") - 1
    copies = column_copies(weight, held, done, ((1, 1), (last, 0)))
    fetches = column_copies(weight, later, later_done, ((1, 0), (last, 1)))
    for n, out in enumerate((ahead_right, behind_left)):
        copies[n].wait()
        product(packed, held[n], out)
    for fetch in fetches:
        fetch.wait()


def join_kernel(packed, kept, up, down, left, right):
    for n, (arrived, out) in enumerate(((up, left), (down, right))):
        own = jnp.dot(packed[...], kept[n], preferred_element_type=jnp.float32)
        own = own.astype(jnp.bfloat16).astype(jnp.float32)
        out[...] = (own + arrived[...].astype(jnp.float32)).astype(jnp.bfloat16)


def own_kernel(packed, weight, from_ahead, from_behind, left, right, held, done):
    copies = column_copies(weight, held, done, ((0, 0), (0, 1)))
    for n, (arrived, out) in enumerate(((from_ahead, left), (from_behind, right))):
        copies[n].wait()
        own = jnp.dot(packed[...], held[n], preferred_element_type=jnp.float32)
        own = own.astype(jnp.bfloat16).astype(jnp.float32)
        out[...] = own + arrived[...].astype(jnp.float32)


def ctx_exchange(x):
    return lax.all_to_all(x, "ctx", split_axis=0, concat_axis=0, tiled=True)


def head_shift(x, by):
    count = lax.axis_size("head")
    return lax.ppermute(x, "head", [(i, (i + by) % count) for i in range(count)])


def wide(x):
    return x.astype(jnp.float32)


def per_device(
    queries,
    keys,
    values,
    out_weight,
    norm_gain,
    tile_counts,
    route_device,
    route_slot,
    session_starts,
):
    ranks = lax.axis_size("ctx")
    groups = lax.axis_size("head")
    rows, width = queries.shape
    heads = width // DH
    part = heads * DH // ranks
    smem = pl.BlockSpec(memory_space=SMEM)
    vmem = pl.BlockSpec(memory_space=VMEM)
    hbm = pl.BlockSpec(memory_space=HBM)
    in_hbm = lambda x: pltpu.with_memory_space_constraint(x, HBM)
    params = pltpu.CompilerParams(vmem_limit_bytes=16 << 20)

    tables = [in_hbm(x) for x in (tile_counts, session_starts, route_device, route_slot)]
    tile_counts, session_starts, route_device, route_slot = tables
    entry, info = pl.pallas_call(
        entry_kernel,
        in_specs=[hbm] * 6,
        out_specs=[vmem, smem],
        out_shape=[
            jax.ShapeDtypeStruct((ranks, part // 2 + 1, 2, DH), jnp.bfloat16),
            jax.ShapeDtypeStruct((8,), jnp.int32),
        ],
        scratch_shapes=[
            pltpu.VMEM((rows, width), keys.dtype),
            pltpu.VMEM((rows, width), values.dtype),
            *[pltpu.SMEM(x.shape, jnp.int32) for x in tables],
            pltpu.SemaphoreType.DMA((2, GROUPS)),
            pltpu.SemaphoreType.DMA((4,)),
        ],
        compiler_params=params,
        name="entry",
    )(*tables, in_hbm(keys), in_hbm(values))

    got = ctx_exchange(entry)

    half = out_weight.shape[1] // groups // 2
    held = lambda n: jax.ShapeDtypeStruct((n, width, half), out_weight.dtype)
    phi_q, inside, resets, route, gain, for_left = pl.pallas_call(
        inside_kernel,
        in_specs=[smem] * 4 + [hbm] * 5,
        out_specs=[vmem] * 2 + [smem] * 2 + [vmem] * 2,
        out_shape=[
            jax.ShapeDtypeStruct((rows, width), jnp.bfloat16),
            jax.ShapeDtypeStruct((rows, width), jnp.bfloat16),
            jax.ShapeDtypeStruct(tile_counts.shape, jnp.int32),
            jax.ShapeDtypeStruct(route_device.shape, jnp.int32),
            jax.ShapeDtypeStruct((1, width), jnp.float32),
            held(1),
        ],
        scratch_shapes=[
            *[pltpu.VMEM((rows, width), jnp.bfloat16)] * 3,
            pltpu.SemaphoreType.DMA((3, GROUPS)),
            pltpu.SemaphoreType.DMA,
            pltpu.SemaphoreType.DMA((1,)),
        ],
        compiler_params=params,
        name="inside",
    )(
        info,
        tile_counts,
        session_starts,
        route_device,
        in_hbm(norm_gain.reshape(1, width)),
        in_hbm(queries),
        in_hbm(keys),
        in_hbm(values),
        in_hbm(out_weight),
    )

    got, phi_q, inside, resets = lax.optimization_barrier((got, phi_q, inside, resets))
    summed, slots, for_right = pl.pallas_call(
        prefix_kernel,
        in_specs=[vmem, vmem, hbm],
        out_specs=[vmem] * 3,
        out_shape=[
            jax.ShapeDtypeStruct((ranks, part // 2, 2, DH), jnp.bfloat16),
            jax.ShapeDtypeStruct((1, DH), jnp.int32),
            held(1),
        ],
        scratch_shapes=[
            pltpu.SMEM(tile_counts.shape, jnp.int32),
            pltpu.SemaphoreType.DMA,
            pltpu.SemaphoreType.DMA((1,)),
        ],
        compiler_params=params,
        name="prefix",
    )(resets, got, in_hbm(out_weight))

    state = ctx_exchange(summed).reshape(heads, DH, DH)

    payload = pl.pallas_call(
        attend_kernel,
        in_specs=[smem] * 2 + [vmem] * 4,
        out_specs=vmem,
        out_shape=jax.ShapeDtypeStruct((ranks, CH, width), jnp.bfloat16),
        scratch_shapes=[pltpu.VMEM((rows, width), jnp.float32)],
        compiler_params=params,
        name="attend",
    )(info, route, phi_q, inside, state, gain)

    arrived = ctx_exchange(payload)

    piece = jax.ShapeDtypeStruct((BAL * CH, half), jnp.bfloat16)
    packed, *across = pl.pallas_call(
        across_kernel,
        in_specs=[smem] + [vmem] * 3,
        out_specs=[vmem] * 3,
        out_shape=[jax.ShapeDtypeStruct((BAL * CH, width), jnp.bfloat16), piece, piece],
        scratch_shapes=[pltpu.SMEM((BAL + 1,), jnp.int32)],
        compiler_params=params,
        name="across",
    )(slots, arrived, for_left, for_right)
    up = head_shift(across[0], 1)
    down = head_shift(across[1], -1)

    ahead_right, behind_left, later = pl.pallas_call(
        beside_kernel,
        in_specs=[vmem, hbm],
        out_specs=[vmem] * 3,
        out_shape=[piece, piece, held(2)],
        scratch_shapes=[
            pltpu.VMEM((2, width, half), out_weight.dtype),
            pltpu.SemaphoreType.DMA((2,)),
            pltpu.SemaphoreType.DMA((2,)),
        ],
        compiler_params=params,
        name="beside",
    )(packed, in_hbm(out_weight))
    from_behind = head_shift(ahead_right, 1)
    from_ahead = head_shift(behind_left, -1)

    left_sum, right_sum = pl.pallas_call(
        join_kernel,
        in_specs=[vmem] * 4,
        out_specs=[vmem] * 2,
        out_shape=[piece] * 2,
        compiler_params=params,
        name="join",
    )(packed, later, up, down)
    last_left = head_shift(left_sum, 1)
    last_right = head_shift(right_sum, -1)

    left, right = pl.pallas_call(
        own_kernel,
        in_specs=[vmem, hbm, vmem, vmem],
        out_specs=[vmem] * 2,
        out_shape=[jax.ShapeDtypeStruct((BAL * CH, half), jnp.float32)] * 2,
        scratch_shapes=[
            pltpu.VMEM((2, width, half), out_weight.dtype),
            pltpu.SemaphoreType.DMA((2,)),
        ],
        compiler_params=params,
        name="own",
    )(packed, in_hbm(out_weight), from_ahead, from_behind)
    left = left + wide(last_left)
    right = right + wide(last_right)
    return jnp.concatenate([left, right], axis=1).astype(jnp.bfloat16)


def solution(mesh):
    placed = (
        P("ctx", "head"),
        P("ctx", "head"),
        P("ctx", "head"),
        P("head", None),
        P("head"),
        P(),
        P("ctx"),
        P("ctx"),
        P(),
    )
    return jax.shard_map(
        per_device, mesh=mesh, in_specs=placed, out_specs=P("ctx", "head"), check_vma=False
    )
```
